256 devices in a mesh: ctx: 64 (over z, y_hi, x), head: 4 (over y_lo, core).
Axes of the slice: x: 4, y: 4 (y_hi: 2, y_lo: 2; y = y_hi * 2 + y_lo), z: 8, core: 2. Of those that a mesh axis runs over, the one named last changes fastest.
Arguments:
- queries: bfloat16 [12288, 4096], P('ctx', 'head'), may hold values from -6 to 6
- attention_keys: bfloat16 [12288, 512], P('ctx'), may hold values from -6 to 6
- attention_values: bfloat16 [12288, 512], P('ctx'), may hold values from -6 to 6
- attn_gate: bfloat16 [12288, 4096], P('ctx', 'head'), may hold values from -6 to 6
- segment_ids: int32 [12288], P('ctx'), may hold values from 0 to 7, never falling along the last dimension, each value on 1 to 3072 neighbouring positions
- value_proj: bfloat16 [4096, 4096], P(None, 'head'), may hold values from -0.09375 to 0.09375
- linear_queries: bfloat16 [12288, 2048], P('ctx', 'head'), may hold values from -6 to 6
- linear_keys: bfloat16 [12288, 2048], P('ctx', 'head'), may hold values from -6 to 6
- conv_queries: bfloat16 [4, 2048], P(None, 'head'), may hold values from -3 to 3
- conv_keys: bfloat16 [4, 2048], P(None, 'head'), may hold values from -3 to 3
- conv_values: bfloat16 [4, 4096], P(None, 'head'), may hold values from -3 to 3
- decay_logits: float32 [12288, 32], P('ctx', 'head'), may hold values from -16 to 0
- beta_logits: float32 [12288, 32], P('ctx', 'head'), may hold values from -16 to 2
- decay_base: float32 [32], P('head'), may hold values from -0.5 to 0.5
- decay_bias: float32 [32], P('head'), may hold values from -0.5 to 0.5
- output_gate: bfloat16 [12288, 4096], P('ctx', 'head'), may hold values from -6 to 6
- output_gain: float32 [128], replicated, may hold values from 0.1 to 1.9
- rezero_gate: float32 [4096], P('head'), may hold values from 0.5 to 1.5
Outputs:
- layer_output: bfloat16 [12288, 4096], P('ctx', 'head')
The draws below stay inside these ranges and needn't reach their ends.
Inputs may be any that keep to these rules, and one draw needn't show every extreme that they name: `segment_ids`: each document spans at most 3072 consecutive tokens, and one spans exactly that many.
All inputs are finite; a program needn't handle non-finite values.
Results may differ from the reference program's by a relative error of at most 0.017.
Values may be sent and summed in bfloat16 or wider, within the bound.
A program may use at most 192 MiB of HBM per device.

```python
import math
import jax
import jax.numpy as jnp
import numpy as np
from jax import lax

QUERY_HEAD_TOTAL = 16
KEY_VALUE_HEADS = 2
HEAD_SIZE = 256
HK = 16
LINEAR_HEADS = 32
DK = 128
DV = 128
KW = 4
TOK_DEV = 192
TOKEN_COUNT = 12288


def draw_queries(key, part):
    random_root_key = jax.random.fold_in(key, 1)
    value_rows = jnp.clip(jax.random.normal(random_root_key, (TOKEN_COUNT, QUERY_HEAD_TOTAL * HEAD_SIZE), jnp.float32), -6.0, 6.0)
    return value_rows.astype(jnp.bfloat16)


def draw_attention_keys(key, part):
    random_root_key = jax.random.fold_in(key, 2)
    value_rows = jnp.clip(jax.random.normal(random_root_key, (TOKEN_COUNT, KEY_VALUE_HEADS * HEAD_SIZE), jnp.float32), -6.0, 6.0)
    return value_rows.astype(jnp.bfloat16)


def draw_decay_logits(key, part):
    head_key = jax.random.fold_in(key, 11)
    device_key = jax.random.fold_in(key, 12)
    token_key = jax.random.fold_in(key, 13)
    spike_random_key = jax.random.fold_in(key, 14)
    fast_heads = jax.random.randint(head_key, (LINEAR_HEADS,), 0, 2) == 0
    roughness = jax.random.uniform(token_key, (TOKEN_COUNT, LINEAR_HEADS), jnp.float32, -1.0, 1.0)
    base_level = jnp.where(fast_heads, math.log(1.0 / 40.0), math.log(0.2 / TOKEN_COUNT)).astype(jnp.float32)
    offsets = jax.random.uniform(device_key, (TOKEN_COUNT // TOK_DEV, LINEAR_HEADS), jnp.float32, -0.5, 0.5)
    offsets = jnp.repeat(offsets, TOK_DEV, axis=0)
    value_rows = base_level[None, :] + offsets + roughness
    spike_draws = jax.random.uniform(spike_random_key, (TOKEN_COUNT, LINEAR_HEADS), jnp.float32) < 4.0 / TOKEN_COUNT
    return jnp.where(spike_draws, -1.0, value_rows)


def draw_beta_logits(key, part):
    random_root_key = jax.random.fold_in(key, 21)
    center = math.log(DK / TOKEN_COUNT)
    spread_draw = jnp.clip(0.5 * jax.random.normal(random_root_key, (TOKEN_COUNT, LINEAR_HEADS), jnp.float32), -1.5, 1.5)
    return center + spread_draw


def level_of(rng, extent, pieces, low, high):
    factor_of = 1.0
    for position, parts in pieces:
        heights = jax.random.uniform(jax.random.fold_in(jax.random.fold_in(rng, 6), position), (parts,), jnp.float32, low / len(pieces), high / len(pieces))
        factor_of = factor_of * jnp.repeat(jnp.exp(heights), extent[position] // parts).reshape((-1,) + (1,) * (len(extent) - 1 - position))
    return factor_of


def split_up(number_of, total, most, slope):
    weights = [(1 << 20) // math.isqrt(grade ** slope) + 1 for grade in range(2, number_of + 1)]
    rest, counts = total - most - (number_of - 1), [1] * (number_of - 1)
    while rest > 0:
        candidates = [i for i in range(number_of - 1) if counts[i] < most]
        pool, budget = sum([weights[i] for i in candidates]), rest
        for i in candidates:
            extra = min(most - counts[i], max(1, budget * weights[i] // pool), rest)
            counts[i] = counts[i] + extra
            rest = rest - extra
    return np.array([most] + counts)


def uneven(rng, number_of, total, most, lean):
    if number_of == 2:
        one = jax.random.randint(rng, (), max(1, total - most), min(most, total - 1) + 1)
        return jnp.stack([one, total - one])
    sizes = jnp.asarray(split_up(number_of, total, most, lean), jnp.int32)
    couples = (number_of - 1) // 2
    donor, taker = sizes[1:1 + 2 * couples:2], sizes[2:2 + 2 * couples:2]
    slack = jnp.minimum(donor - 1, most - taker)
    moved = jax.random.randint(jax.random.fold_in(rng, 1), (couples,), 0, 1 << 20) % (slack + 1)
    sizes = sizes.at[1:1 + 2 * couples:2].set(donor - moved).at[2:2 + 2 * couples:2].set(taker + moved)
    return sizes[jax.random.permutation(jax.random.fold_in(rng, 2), number_of)]


def scatter_about(rng, extent, scale, limit, shards=(), held_as=jnp.bfloat16):
    gain = level_of(rng, extent, shards, -0.22, 0.18) if shards else 1.0
    result = jax.random.normal(rng, extent, jnp.float32) * scale * gain
    return jnp.minimum(jnp.maximum(result, -limit), limit).astype(held_as)


def setup_inputs(seed: int = 0) -> dict:
    splits = jax.random.split(jax.random.key(seed), 19)
    queries = draw_queries(jax.random.fold_in(splits[18], 71), 0)
    attention_keys = draw_attention_keys(jax.random.fold_in(splits[18], 71), 0)
    attention_values = scatter_about(splits[2], (TOKEN_COUNT, KEY_VALUE_HEADS * HEAD_SIZE), 1.0, 6.0, ((0, 64),))
    attn_gate = scatter_about(splits[3], (TOKEN_COUNT, QUERY_HEAD_TOTAL * HEAD_SIZE), 1.0, 6.0, ((0, 64), (1, 4)))
    segment_ids = jnp.searchsorted(jnp.cumsum(uneven(splits[4], 8, TOKEN_COUNT, TOKEN_COUNT // 4, 2)), jnp.arange(TOKEN_COUNT), side="right").astype(jnp.int32)
    value_proj = scatter_about(splits[5], (QUERY_HEAD_TOTAL * HEAD_SIZE, LINEAR_HEADS * DV), (QUERY_HEAD_TOTAL * HEAD_SIZE) ** -0.5, 0.09375, ((1, 4),))
    linear_queries = scatter_about(splits[6], (TOKEN_COUNT, HK * DK), 1.0, 6.0, ((0, 64), (1, 4)))
    linear_keys = scatter_about(splits[7], (TOKEN_COUNT, HK * DK), 1.0, 6.0, ((0, 64), (1, 4)))
    conv_queries = scatter_about(splits[8], (KW, HK * DK), KW ** -0.5, 3.0, ((1, 4),))
    conv_keys = scatter_about(splits[9], (KW, HK * DK), KW ** -0.5, 3.0, ((1, 4),))
    conv_values = scatter_about(splits[10], (KW, LINEAR_HEADS * DV), KW ** -0.5, 3.0, ((1, 4),))
    decay_logits = draw_decay_logits(jax.random.fold_in(splits[18], 71), 0)
    beta_logits = draw_beta_logits(jax.random.fold_in(splits[18], 71), 0)
    decay_base = jnp.clip(jax.random.uniform(splits[13], (LINEAR_HEADS,), jnp.float32, -0.5, 0.5) * level_of(splits[13], (LINEAR_HEADS,), ((0, 4),), -0.4, 0.0), -0.5, 0.5)
    decay_bias = jnp.clip(jax.random.uniform(splits[14], (LINEAR_HEADS,), jnp.float32, -0.5, 0.5) * level_of(splits[14], (LINEAR_HEADS,), ((0, 4),), -0.4, 0.0), -0.5, 0.5)
    output_gate = scatter_about(splits[15], (TOKEN_COUNT, LINEAR_HEADS * DV), 1.0, 6.0, ((0, 64), (1, 4)))
    output_gain = jnp.clip(1.0 + 0.18 * jax.random.normal(splits[16], (DV,), jnp.float32), 0.1, 1.9)
    rezero_gate = jnp.clip(0.5 + 1.0 * jax.random.uniform(splits[17], (LINEAR_HEADS * DV,), jnp.float32) ** level_of(splits[17], (LINEAR_HEADS * DV,), ((0, 4),), -0.2, 0.2), 0.5, 1.5)
    return dict(queries=queries, attention_keys=attention_keys, attention_values=attention_values, attn_gate=attn_gate, segment_ids=segment_ids, value_proj=value_proj, linear_queries=linear_queries, linear_keys=linear_keys, conv_queries=conv_queries, conv_keys=conv_keys, conv_values=conv_values, decay_logits=decay_logits, beta_logits=beta_logits, decay_base=decay_base, decay_bias=decay_bias, output_gate=output_gate, output_gain=output_gain, rezero_gate=rezero_gate)


EPSILON = 1e-06
FINEST_ACCURACY = lax.Precision.HIGHEST

def causal_conv(inputs, taps):
    sequence_length = inputs.shape[0]
    tap_count = taps.shape[0]
    padded = jnp.concatenate([jnp.zeros((tap_count - 1, inputs.shape[1]), jnp.float32), inputs.astype(jnp.float32)], axis=0)
    taps_wide = taps.astype(jnp.float32)
    summed = jnp.zeros((sequence_length, inputs.shape[1]), jnp.float32)
    for tap_index in range(tap_count):
        summed = summed + taps_wide[tap_index] * padded[tap_index:tap_index + sequence_length]
    return jax.nn.silu(summed)

def unit_rows(tensor):
    return tensor / jnp.sqrt(lax.optimization_barrier(jnp.sum(tensor * tensor, axis=-1, keepdims=True)) + EPSILON)

def reference(queries, attention_keys, attention_values, attn_gate, segment_ids, value_proj, linear_queries, linear_keys, conv_queries, conv_keys, conv_values, decay_logits, beta_logits, decay_base, decay_bias, output_gate, output_gain, rezero_gate):
    sequence_length = queries.shape[0]
    group_width = QUERY_HEAD_TOTAL // KEY_VALUE_HEADS
    block_rows = math.gcd(sequence_length, 256)
    block_total = sequence_length // block_rows
    query_sequence = queries.astype(jnp.float32).reshape(sequence_length, KEY_VALUE_HEADS, group_width, HEAD_SIZE)
    key_sequence = attention_keys.astype(jnp.float32).reshape(sequence_length, KEY_VALUE_HEADS, HEAD_SIZE)
    value_sequence = attention_values.astype(jnp.float32).reshape(sequence_length, KEY_VALUE_HEADS, HEAD_SIZE)
    positions = jnp.arange(sequence_length, dtype=jnp.int32)

    def attend(index):
        first_row = index * block_rows
        query_block = lax.dynamic_slice_in_dim(query_sequence, first_row, block_rows, 0)
        query_pos = first_row + jnp.arange(block_rows, dtype=jnp.int32)
        query_seg = lax.dynamic_slice_in_dim(segment_ids, first_row, block_rows, 0)
        scores = jnp.einsum('qcgd,kcd->cgqk', query_block, key_sequence) / math.sqrt(HEAD_SIZE)
        allowed = (positions[None, :] <= query_pos[:, None]) & (segment_ids[None, :] == query_seg[:, None])
        scores = jnp.where(allowed, scores, -1e+30)
        row_max = lax.optimization_barrier(jnp.max(scores, axis=-1, keepdims=True))
        weights = jnp.where(allowed, jnp.exp(scores - row_max), 0.0)
        row_total = lax.optimization_barrier(jnp.sum(weights, axis=-1))
        rounded = lax.optimization_barrier(weights.astype(jnp.bfloat16)).astype(jnp.float32)
        summed = jnp.einsum('cgqk,kcd->qcgd', rounded, value_sequence)
        return summed / jnp.transpose(row_total, (2, 0, 1))[..., None]
    attended = lax.map(attend, jnp.arange(block_total, dtype=jnp.int32)).reshape(sequence_length, QUERY_HEAD_TOTAL * HEAD_SIZE)
    attn_out = (jax.nn.sigmoid(attn_gate.astype(jnp.float32)) * attended).astype(jnp.bfloat16)
    mean_square = lax.optimization_barrier(jnp.mean(jnp.square(attn_out.astype(jnp.float32)), axis=-1, keepdims=True))
    projected = jnp.dot(attn_out, value_proj, preferred_element_type=jnp.float32)
    value_in = (projected / jnp.sqrt(mean_square + EPSILON)).astype(jnp.bfloat16)
    conv_q = causal_conv(linear_queries, conv_queries).reshape(sequence_length, HK, DK)
    conv_k = causal_conv(linear_keys, conv_keys).reshape(sequence_length, HK, DK)
    conv_v = causal_conv(value_in, conv_values).reshape(sequence_length, LINEAR_HEADS, DV)
    lin_q = unit_rows(conv_q) / math.sqrt(DK)
    lin_k = unit_rows(conv_k)
    repeat = LINEAR_HEADS // HK
    query_heads = jnp.repeat(lin_q, repeat, axis=1)
    key_heads = jnp.repeat(lin_k, repeat, axis=1)
    log_decay = -jnp.exp(decay_base)[None, :] * jax.nn.softplus(decay_logits + decay_bias[None, :])
    beta = jax.nn.sigmoid(beta_logits)

    def advance(memory_operator, inputs):
        query_current, present_address_vector, present_content_vector, decay_now, step_write_strength = inputs
        memory_operator = jnp.exp(decay_now)[:, None, None] * memory_operator
        predicted_outputs = jnp.einsum('pdj,pd->pj', memory_operator, present_address_vector, precision=FINEST_ACCURACY)
        memory_operator = memory_operator + step_write_strength[:, None, None] * present_address_vector[:, :, None] * (present_content_vector - predicted_outputs)[:, None, :]
        return (memory_operator, jnp.einsum('pdj,pd->pj', memory_operator, query_current, precision=FINEST_ACCURACY))
    final_state, delta_out = lax.scan(advance, jnp.zeros((LINEAR_HEADS, DK, DV), jnp.float32), (query_heads, key_heads, conv_v, log_decay, beta))
    gate_heads = jax.nn.silu(output_gate.astype(jnp.float32).reshape(sequence_length, LINEAR_HEADS, DV))
    normalized = delta_out / jnp.sqrt(lax.optimization_barrier(jnp.mean(delta_out * delta_out, axis=-1, keepdims=True)) + EPSILON)
    gated_out = normalized * output_gain[None, None, :] * gate_heads
    mixed_sum = attn_out.astype(jnp.float32) + rezero_gate[None, :] * gated_out.reshape(sequence_length, LINEAR_HEADS * DV)
    return mixed_sum.astype(jnp.bfloat16)
```

```python
import functools

import jax
import jax.numpy as jnp
from jax import lax
from jax.experimental import pallas as pl
from jax.experimental.pallas import tpu as pltpu
from jax.sharding import PartitionSpec as P

MESH = pl.DeviceIdType.MESH
EPSILON = 1e-06
NEGATIVE = -1e30
HIGH = lax.Precision.HIGHEST
F32 = jnp.float32
BF16 = jnp.bfloat16

ROWS = 192
HALF = 96
WINDOW = 17
HEADS = 8


def coords():
    ctx = lax.axis_index("ctx")
    head = lax.axis_index("head")
    z, place = lax.div(ctx, 8), lax.rem(ctx, 8)
    y_hi, x = lax.div(place, 4), lax.rem(place, 4)
    y_lo, core = lax.div(head, 2), lax.rem(head, 2)
    return ctx, head, z, place, y_hi, x, y_lo, core


def greet(sources):
    barrier = pltpu.get_barrier_semaphore()
    for device in sources:
        pl.semaphore_signal(barrier, inc=1, device_id=device, device_id_type=MESH)
    pl.semaphore_wait(barrier, len(sources))


def push(src, dst, send_sem, recv_sem, device):
    return pltpu.make_async_remote_copy(
        src_ref=src,
        dst_ref=dst,
        send_sem=send_sem,
        recv_sem=recv_sem,
        device_id=device,
        device_id_type=MESH,
    )


def window_kernel(
    keys, values, seg, kv, segs, own, own_seg, load_sem, y_s, y_r, z_s, z_r, x_s, x_r, f_s, f_r
):
    ctx, head, z, place, y_hi, x, y_lo, core = coords()
    partner = (ctx, y_lo * 2 + 1 - core)
    across = (z * 8 + (1 - y_hi) * 4 + x, (1 - y_lo) * 2 + core)
    above = (lax.rem(z + 1, 8) * 8 + place, head)
    below = (lax.rem(z + 7, 8) * 8 + place, head)
    beside = [(z * 8 + y_hi * 4 + lax.rem(x + d, 4), head) for d in (1, 3, 2)]
    rows = pl.ds(pl.multiple_of(core * HALF, 16), HALF)
    mine = pl.ds(pl.multiple_of(y_lo * 256, 256), 256)
    other = pl.ds(pl.multiple_of((1 - y_lo) * 256, 256), 256)

    local = [
        pltpu.make_async_copy(keys.at[:, mine], own.at[0, :, pl.ds(0, 256)], load_sem.at[0]),
        pltpu.make_async_copy(values.at[:, mine], own.at[0, :, pl.ds(256, 256)], load_sem.at[1]),
        pltpu.make_async_copy(keys.at[rows, other], own.at[1, rows, pl.ds(0, 256)], load_sem.at[2]),
        pltpu.make_async_copy(
            values.at[rows, other], own.at[1, rows, pl.ds(256, 256)], load_sem.at[3]
        ),
        pltpu.make_async_copy(seg, own_seg, load_sem.at[4]),
    ]
    for copy in local:
        copy.start()
    greet([partner, across, below] + beside)
    for copy in local:
        copy.wait()
    keep = [
        pltpu.make_async_copy(own.at[0], kv.at[0, y_hi, x], load_sem.at[5]),
        pltpu.make_async_copy(own_seg, segs.at[x, 0, y_hi], load_sem.at[6]),
    ]
    for copy in keep:
        copy.start()

    y_copy = [
        push(own.at[1, rows], kv.at[0, y_hi, x, rows], y_s.at[0], y_r.at[0], across),
        push(own_seg, segs.at[x, 0, y_hi], y_s.at[1], y_r.at[1], across),
    ]
    for copy in y_copy:
        copy.start()
    y_back = [
        push(own.at[1, rows], kv.at[0, 1 - y_hi, x, rows], y_s.at[0], y_r.at[0], across),
        push(own_seg, segs.at[x, 0, 1 - y_hi], y_s.at[1], y_r.at[1], across),
    ]

    def z_push(step, yh, index):
        return push(
            kv.at[step, yh, x, rows], kv.at[step + 1, yh, x, rows], z_s.at[index], z_r.at[index], above
        )

    def forward(step, yh, xs, index):
        return push(
            kv.at[step, yh, xs, rows], kv.at[step, yh, xs, rows], f_s.at[index], f_r.at[index], partner
        )

    def forwarded(step, yh, xs, index):
        back = pl.ds(pl.multiple_of((1 - core) * HALF, 16), HALF)
        return push(
            kv.at[step, yh, xs, back], kv.at[step, yh, xs, back], f_s.at[index], f_r.at[index], partner
        )

    z_first = push(own.at[0, rows], kv.at[1, y_hi, x, rows], z_s.at[0], z_r.at[0], above)
    z_first.start()

    def x_push(k, step, yh, index, src=None):
        source = kv.at[step, yh, x, rows] if src is None else src
        return push(source, kv.at[step, yh, x, rows], x_s.at[k, index], x_r.at[k, index], beside[k])

    def later(k, yh):
        dest = y_hi * 4 + lax.rem(x + (1, 3, 2)[k], 4)
        return yh * 4 + x < dest

    for k in range(3):
        early = later(k, y_hi)

        @pl.when(early)
        def _(k=k):
            x_push(k, 0, y_hi, 0, own.at[0, rows]).start()

    for copy in y_back:
        copy.wait_recv()
    z_second = z_push(0, 1 - y_hi, 1)
    z_second.start()
    z_seg = push(segs.at[x, 0], segs.at[x, 1], z_s.at[4], z_r.at[4], above)
    keep[1].wait()
    z_seg.start()
    for k in range(3):
        early = later(k, 1 - y_hi)

        @pl.when(early)
        def _(k=k):
            x_push(k, 0, 1 - y_hi, 1).start()

    forwards = [(0, 1 - y_hi, x)]
    forward(*forwards[0], 0).start()

    for yh, index in ((y_hi, 0), (1 - y_hi, 1)):
        z_push(0, yh, index).wait_recv()
        z_push(1, yh, 2 + index).start()
        for k in range(3):
            x_push(k, 1, yh, 2 + index).start()
        forward(1, yh, x, len(forwards)).start()
        forwards.append((1, yh, x))
    z_seg.wait_recv()
    z_seg_on = push(segs.at[x, 1], segs.at[x, 2], z_s.at[5], z_r.at[5], above)
    z_seg_on.start()
    for yh, index in ((y_hi, 0), (1 - y_hi, 1)):
        z_push(1, yh, 2 + index).wait_recv()
        for k in range(3):
            late = jnp.logical_not(later(k, yh))

            @pl.when(late)
            def _(k=k, yh=yh, index=index):
                x_push(k, 2, yh, index).start()

        forward(2, yh, x, len(forwards)).start()
        forwards.append((2, yh, x))
    z_seg_on.wait_recv()
    x_seg = [
        push(segs.at[x], segs.at[x], x_s.at[k, 4], x_r.at[k, 4], beside[k]) for k in range(3)
    ]
    for copy in x_seg:
        copy.start()

    def came(k, step, yh, index):
        xs = lax.rem(x + (3, 1, 2)[k], 4)
        return push(
            kv.at[step, yh, xs, rows], kv.at[step, yh, xs, rows], x_s.at[k, index], x_r.at[k, index], beside[k]
        )

    def choice(k, yh):
        xs = lax.rem(x + (3, 1, 2)[k], 4)
        return jnp.where(yh * 4 + xs < place, 0, 2)

    for k in range(3):
        xs = lax.rem(x + (3, 1, 2)[k], 4)
        for yh, index in ((y_hi, 0), (1 - y_hi, 1)):
            came(k, 1, yh, 2 + index).wait_recv()
            forward(1, yh, xs, len(forwards)).start()
            forwards.append((1, yh, xs))
    for k in range(3):
        xs = lax.rem(x + (3, 1, 2)[k], 4)
        for yh, index in ((y_hi, 0), (1 - y_hi, 1)):
            step = choice(k, yh)
            came(k, step, yh, index).wait_recv()
            forward(step, yh, xs, len(forwards)).start()
            forwards.append((step, yh, xs))
        x_seg_in = push(segs.at[xs], segs.at[xs], x_s.at[k, 4], x_r.at[k, 4], beside[k])
        x_seg_in.wait_recv()
    for index, where in enumerate(forwards):
        forwarded(*where, index).wait_recv()
    keep[0].wait()
    for copy in y_copy:
        copy.wait_send()
    z_first.wait_send()
    z_second.wait_send()
    z_seg.wait_send()
    z_seg_on.wait_send()
    for index in (2, 3):
        z_push(1, y_hi, index).wait_send()
    for k in range(3):
        for index in range(4):
            x_push(k, 1, y_hi, index).wait_send()
        x_seg[k].wait_send()
    for index, where in enumerate(forwards):
        forward(*where, index).wait_send()


def window(keys, values, seg_tile):
    dma = pltpu.SemaphoreType.DMA
    return pl.pallas_call(
        window_kernel,
        out_shape=(
            jax.ShapeDtypeStruct((3, 2, 4, ROWS, 512), BF16),
            jax.ShapeDtypeStruct((4, 3, 2, 8, 128), jnp.int32),
        ),
        in_specs=[pl.BlockSpec(memory_space=pl.ANY)] * 3,
        out_specs=[pl.BlockSpec(memory_space=pl.ANY)] * 2,
        scratch_shapes=[
            pltpu.VMEM((2, ROWS, 512), BF16),
            pltpu.VMEM((8, 128), jnp.int32),
            dma((7,)),
            dma((2,)),
            dma((2,)),
            dma((6,)),
            dma((6,)),
            dma((3, 5)),
            dma((3, 5)),
            dma((17,)),
            dma((17,)),
        ],
        compiler_params=pltpu.CompilerParams(collective_id=0, has_side_effects=True),
        name="window_of_keys",
    )(keys, values, seg_tile)


def attention_kernel(slots, kv, segs, seg_query, queries, gate, out, q_all, first, m_sc, l_sc, acc):
    step = pl.program_id(0)
    lanes = 4 * ROWS

    @pl.when(step == 0)
    def _():
        for h in range(4):
            q_all[h * ROWS : (h + 1) * ROWS, :] = (
                queries[:, h * 256 : (h + 1) * 256].astype(F32) * 0.0625
            ).astype(BF16)
        m_sc[...] = jnp.full(m_sc.shape, NEGATIVE, F32)
        l_sc[...] = jnp.zeros(l_sc.shape, F32)
        acc[...] = jnp.zeros(acc.shape, F32)
        begin = jnp.zeros((1, lanes), jnp.int32)
        missing = slots[2 * WINDOW]
        for doc in range(8):
            less = jnp.zeros((8, 128), jnp.int32)
            for b in range(WINDOW):
                block = segs[slots[WINDOW + b]]
                less = less + jnp.where((block < doc) & (b >= missing), 1, 0)
            total = jnp.sum(less) + missing * ROWS
            begin = jnp.where(seg_query[...] == doc, total, begin)
        first[...] = jnp.broadcast_to(begin, first.shape)

    block = lax.rem(WINDOW - 1 + step, WINDOW)
    keys, values = kv[0, :, 0:256], kv[0, :, 256:512]
    scores = lax.dot_general(
        keys, q_all[...], (((1,), (1,)), ((), ())), preferred_element_type=F32
    )
    key_pos = block * ROWS + lax.broadcasted_iota(jnp.int32, (ROWS, lanes), 0)
    token = lax.broadcasted_iota(jnp.int32, (1, lanes), 1)
    for h in range(1, 4):
        token = jnp.where(token >= ROWS, token - ROWS, token)
    last = (WINDOW - 1) * ROWS + token
    allowed = (key_pos >= first[0:1, :]) & (key_pos <= last)
    scores = jnp.where(allowed, scores, NEGATIVE)
    m_old = m_sc[0:1, :]
    m_new = jnp.maximum(m_old, jnp.max(scores, axis=0, keepdims=True))
    scale = jnp.exp(m_old - m_new)
    weights = jnp.exp(scores - m_new)
    l_sc[0:1, :] = l_sc[0:1, :] * scale + jnp.sum(weights, axis=0, keepdims=True)
    m_sc[0:1, :] = m_new
    added = lax.dot_general(
        values, weights.astype(BF16), (((0,), (0,)), ((), ())), preferred_element_type=F32
    )
    acc[...] = acc[...] * scale + added

    @pl.when(step == WINDOW - 1)
    def _():
        mean = jnp.transpose(acc[...] / l_sc[0:1, :])
        for h in range(4):
            g = gate[:, h * 256 : (h + 1) * 256].astype(F32)
            out[:, h * 256 : (h + 1) * 256] = (
                jax.nn.sigmoid(g) * mean[h * ROWS : (h + 1) * ROWS, :]
            ).astype(BF16)


def attention(slots, kv, segs, seg_query, queries, gate):
    full = lambda shape: pl.BlockSpec(shape, lambda s, slots: (0,) * len(shape))
    lanes = 4 * ROWS
    return pl.pallas_call(
        attention_kernel,
        out_shape=jax.ShapeDtypeStruct((ROWS, 1024), BF16),
        grid_spec=pltpu.PrefetchScalarGridSpec(
            num_scalar_prefetch=1,
            grid=(WINDOW,),
            in_specs=[
                pl.BlockSpec(
                    (1, ROWS, 512),
                    lambda s, slots: (slots[lax.rem(WINDOW - 1 + s, WINDOW)], 0, 0),
                ),
                full((24, 8, 128)),
                full((1, lanes)),
                full((ROWS, 1024)),
                full((ROWS, 1024)),
            ],
            out_specs=full((ROWS, 1024)),
            scratch_shapes=[
                pltpu.VMEM((lanes, 256), BF16),
                pltpu.VMEM((8, lanes), jnp.int32),
                pltpu.VMEM((8, lanes), F32),
                pltpu.VMEM((8, lanes), F32),
                pltpu.VMEM((256, lanes), F32),
            ],
        ),
        name="window_attention",
    )(slots, kv, segs, seg_query, queries, gate)


PIECES = 3


def heads_kernel(own, out, l_sem, p_s, p_r, a_s, a_r, f_s, f_r):
    ctx, head, z, place, y_hi, x, y_lo, core = coords()
    partner = (ctx, y_lo * 2 + 1 - core)
    across = (ctx, (1 - y_lo) * 2 + core)
    greet([partner, across])
    size = ROWS // PIECES

    def part(i, h):
        return out.at[pl.ds(i * size, size), pl.ds(pl.multiple_of(h * 1024, 1024), 1024)]

    def piece(i):
        return own.at[pl.ds(i * size, size)]

    far, farther = (1 - y_lo) * 2 + core, (1 - y_lo) * 2 + 1 - core
    keep = [pltpu.make_async_copy(piece(i), part(i, head), l_sem.at[i]) for i in range(PIECES)]
    for i in range(PIECES):
        push(piece(i), part(i, head), a_s.at[i], a_r.at[i], across).start()
        push(piece(i), part(i, head), p_s.at[i], p_r.at[i], partner).start()
        keep[i].start()
    for i in range(PIECES):
        push(piece(i), part(i, far), a_s.at[i], a_r.at[i], across).wait_recv()
        push(part(i, far), part(i, far), f_s.at[i], f_r.at[i], partner).start()
    for i in range(PIECES):
        near = y_lo * 2 + 1 - core
        push(piece(i), part(i, near), p_s.at[i], p_r.at[i], partner).wait()
        push(part(i, far), part(i, farther), f_s.at[i], f_r.at[i], partner).wait()
        push(piece(i), part(i, far), a_s.at[i], a_r.at[i], across).wait_send()
        keep[i].wait()


def all_heads(own):
    dma = pltpu.SemaphoreType.DMA
    return pl.pallas_call(
        heads_kernel,
        out_shape=jax.ShapeDtypeStruct((ROWS, 4096), BF16),
        in_specs=[pl.BlockSpec(memory_space=pltpu.VMEM)],
        out_specs=pl.BlockSpec(memory_space=pl.ANY),
        scratch_shapes=[dma((PIECES,))] * 7,
        compiler_params=pltpu.CompilerParams(collective_id=1, has_side_effects=True),
        name="all_heads",
    )(own)


def mm(a, b, precision=None):
    return jnp.dot(a, b, precision=precision, preferred_element_type=F32)


def mm_t(a, b, precision=None):
    return lax.dot_general(
        a, b, (((1,), (1,)), ((), ())), precision=precision, preferred_element_type=F32
    )


def causal(ext, taps, width):
    total = jnp.zeros((ROWS, width), F32)
    for m in range(4):
        total = total + taps[m : m + 1, :] * ext[13 + m : 13 + m + ROWS, 0:width]
    return total / (1.0 + jnp.exp(-total))


def triangle(size, strict):
    row = lax.broadcasted_iota(jnp.int32, (size, size), 0)
    col = lax.broadcasted_iota(jnp.int32, (size, size), 1)
    return (col < row) if strict else (col <= row)


def inverse_lower(system, work):
    row = lax.broadcasted_iota(jnp.int32, (ROWS, ROWS), 0)
    col = lax.broadcasted_iota(jnp.int32, (ROWS, ROWS), 1)
    unit = jnp.where(row == col, 1.0, 0.0)
    power = jnp.where(lax.div(row, 8) == lax.div(col, 8), -system, 0.0)
    inverse = unit + power
    for _ in range(2):
        power = mm(power, power, HIGH)
        inverse = inverse + mm(inverse, power, HIGH)
    size = 8
    while size < ROWS:
        pair = 2 * size
        below = (lax.div(row, pair) == lax.div(col, pair)) & (lax.div(row, size) != lax.div(col, size))
        if pair >= ROWS:
            below = lax.div(row, size) != lax.div(col, size)
        joint = jnp.where(below, system, 0.0)
        inverse = inverse - mm(inverse, mm(joint, inverse, HIGH), HIGH)
        size = pair
    return inverse


def linear_kernel(
    lq, lk, cq, ck, decay, beta, h_out, eff_out, g_out, px_out, mz_out,
    halo, ext, q_sc, k_sc, t_own, t_all, row_sc, p_own, p_all,
    hs, hr, ts, tr, zs, zr,
):
    ctx, head, z, place, y_hi, x, y_lo, core = coords()
    following = (lax.rem(ctx + 1, 64), head)
    previous = (lax.rem(ctx + 63, 64), head)
    plane = [(z * 8 + lax.rem(place + d, 8), head) for d in range(1, 8)]
    column = [(lax.rem(z + d, 8) * 8 + place, head) for d in range(1, 8)]
    greet([previous] + plane + column)
    tail = pl.ds(ROWS - 16, 16)
    edge = [
        push(lq.at[tail], halo.at[0], hs.at[0], hr.at[0], following),
        push(lk.at[tail], halo.at[1], hs.at[1], hr.at[1], following),
    ]
    for copy in edge:
        copy.start()
    for copy in edge:
        copy.wait()
    begins = ctx == 0
    for source, taps, index, target in ((lq, cq, 0, q_sc), (lk, ck, 1, k_sc)):
        ext[0:16, :] = jnp.where(begins, 0.0, halo[index].astype(F32))
        ext[16 : 16 + ROWS, :] = source[...].astype(F32)
        conv = causal(ext, taps, 512)
        for n in range(4):
            part = conv[:, n * 128 : (n + 1) * 128]
            part = part / jnp.sqrt(jnp.sum(part * part, axis=1, keepdims=True) + EPSILON)
            if index == 0:
                part = part * (1.0 / 128.0**0.5)
            target[n] = part
    lower = triangle(ROWS, False)
    strict = triangle(ROWS, True)
    ones = jnp.where(lower, 1.0, 0.0)
    row = lax.broadcasted_iota(jnp.int32, (ROWS, ROWS), 0)
    col = lax.broadcasted_iota(jnp.int32, (ROWS, ROWS), 1)
    unit = jnp.where(row == col, 1.0, 0.0)
    unit_k = jnp.where(
        lax.broadcasted_iota(jnp.int32, (128, 128), 0)
        == lax.broadcasted_iota(jnp.int32, (128, 128), 1),
        1.0,
        0.0,
    )
    sum_row = mm_t(decay[...], ones, HIGH)
    sum_col = mm_t(ones, decay[...], HIGH)
    beta_col = mm_t(unit, beta[...], HIGH)
    for e in range(HEADS):
        q, k = q_sc[e // 2], k_sc[e // 2]
        if e % 2 == 0:
            key_key = mm_t(k, k, HIGH)
            query_key = mm_t(q, k, HIGH)
        c_col, c_row = sum_col[:, e : e + 1], sum_row[e : e + 1, :]
        b_col, b_row = beta_col[:, e : e + 1], beta[e : e + 1, :]
        fade = jnp.exp(jnp.where(lower, c_col - c_row, NEGATIVE))
        system = jnp.where(strict, b_col * key_key * fade, 0.0)
        inverse = inverse_lower(system, None)
        grown = jnp.exp(c_col)
        weight_keys = mm(inverse, (b_col * grown) * k, HIGH)
        scores = query_key * fade
        eff = grown * q - mm(scores, weight_keys, HIGH)
        eff_out[e] = eff.astype(BF16)
        h_out[e] = (mm(scores, inverse, HIGH) * b_row).astype(BF16)
        final = c_col[ROWS - 1 : ROWS, :]
        decayed = jnp.transpose(jnp.exp(final - c_col) * k)
        t_own[e] = (jnp.exp(final) * unit_k - mm(decayed, weight_keys, HIGH)).astype(BF16)
        g_out[e] = (mm(decayed, inverse, HIGH) * b_row).astype(BF16)

    sends = []
    for d in range(1, 8):
        owner = lax.rem(place + d, 8)
        copy = push(t_own.at[owner], t_all.at[8 - d], ts.at[d - 1], tr.at[7 - d], plane[d - 1])
        copy.start()
        sends.append(copy)
    t_all[0] = t_own[place]
    for d in range(1, 8):
        push(t_own.at[0], t_all.at[8 - d], ts.at[d - 1], tr.at[7 - d], plane[d - 1]).wait_recv()
    row_sc[...] = jnp.zeros(row_sc.shape, F32)
    row_sc[:, 0:128] = unit_k
    px_out[0] = row_sc[...].astype(BF16)
    for i in range(8):
        current = t_all[lax.rem(i - place + 8, 8)].astype(F32)
        width = (i + 1) * 128
        row_sc[:, 0:width] = mm(current, row_sc[:, 0:width], HIGH)
        row_sc[:, width : width + 128] = unit_k
        px_out[i + 1] = row_sc[...].astype(BF16)
    p_own[...] = row_sc[:, 0:128].astype(BF16)
    for d in range(1, 8):
        copy = push(p_own, p_all.at[d - 1], zs.at[d - 1], zr.at[d - 1], column[d - 1])
        copy.start()
        sends.append(copy)
    for d in range(1, 8):
        push(p_own, p_all.at[d - 1], zs.at[d - 1], zr.at[d - 1], column[d - 1]).wait_recv()
    running = unit_k
    for r in range(1, 8):
        valid = z >= r
        mz_out[:, (r - 1) * 128 : r * 128] = jnp.where(valid, running, 0.0).astype(BF16)
        if r < 7:
            running = mm(running, p_all[r - 1].astype(F32), HIGH)
    for copy in sends:
        copy.wait_send()


def linear(lq, lk, cq, ck, decay, beta):
    dma = pltpu.SemaphoreType.DMA
    vmem = pl.BlockSpec(memory_space=pltpu.VMEM)
    return pl.pallas_call(
        linear_kernel,
        out_shape=(
            jax.ShapeDtypeStruct((HEADS, ROWS, ROWS), BF16),
            jax.ShapeDtypeStruct((HEADS, ROWS, 128), BF16),
            jax.ShapeDtypeStruct((HEADS, 128, ROWS), BF16),
            jax.ShapeDtypeStruct((9, 128, 1152), BF16),
            jax.ShapeDtypeStruct((128, 896), BF16),
        ),
        in_specs=[vmem] * 6,
        out_specs=[vmem] * 5,
        scratch_shapes=[
            pltpu.VMEM((2, 16, 512), BF16),
            pltpu.VMEM((16 + ROWS, 512), F32),
            pltpu.VMEM((4, ROWS, 128), F32),
            pltpu.VMEM((4, ROWS, 128), F32),
            pltpu.VMEM((8, 128, 128), BF16),
            pltpu.VMEM((8, 128, 128), BF16),
            pltpu.VMEM((128, 1152), F32),
            pltpu.VMEM((128, 128), BF16),
            pltpu.VMEM((7, 128, 128), BF16),
            dma((2,)),
            dma((2,)),
            dma((7,)),
            dma((7,)),
            dma((7,)),
            dma((7,)),
        ],
        compiler_params=pltpu.CompilerParams(collective_id=2, has_side_effects=True),
        name="linear_operators",
    )(lq, lk, cq, ck, decay, beta)


def delta_kernel(
    value_in, cv, h_in, eff_in, g_in, px_in, mz_in, attn, gate, gain, rezero, out,
    halo, ext, v_sc, b_own, b_all, local, l_own, l_all, within, s_own, s_all,
    hs, hr, bs, br, zs, zr, ss, sr,
):
    ctx, head, z, place, y_hi, x, y_lo, core = coords()
    following = (lax.rem(ctx + 1, 64), head)
    previous = (lax.rem(ctx + 63, 64), head)
    plane = [(z * 8 + lax.rem(place + d, 8), head) for d in range(1, 8)]
    column = [(lax.rem(z + d, 8) * 8 + place, head) for d in range(1, 8)]
    greet([previous] + plane + column)
    edge = push(value_in.at[pl.ds(ROWS - 16, 16)], halo, hs.at[0], hr.at[0], following)
    edge.start()
    ext[16 : 16 + ROWS, :] = value_in[...].astype(F32)
    edge.wait()
    ext[0:16, :] = jnp.where(ctx == 0, 0.0, halo[...].astype(F32))
    v_sc[...] = causal(ext, cv, 1024).astype(BF16)
    for e in range(HEADS):
        b_own[e] = mm(g_in[e], v_sc[:, e * 128 : (e + 1) * 128]).astype(BF16)
    sends = []
    for d in range(1, 8):
        owner = lax.rem(place + d, 8)
        copy = push(b_own.at[owner], b_all.at[place], bs.at[d - 1], br.at[d - 1], plane[d - 1])
        copy.start()
        sends.append(copy)
    b_all[place] = b_own[place]
    for e in range(HEADS):
        local[e] = mm(h_in[e], v_sc[:, e * 128 : (e + 1) * 128])
    for d in range(1, 8):
        source = lax.rem(place + 8 - d, 8)
        push(b_own.at[0], b_all.at[source], bs.at[d - 1], br.at[d - 1], plane[d - 1]).wait_recv()
    blocks = b_all[...].reshape(8 * 128, 128)
    l_own[...] = mm(px_in[8, :, 128:1152], blocks).astype(BF16)
    for d in range(1, 8):
        copy = push(l_own, l_all.at[d - 1], zs.at[d - 1], zr.at[d - 1], column[d - 1])
        copy.start()
        sends.append(copy)
    for i in range(8):
        within[i] = mm(px_in[i, :, 128:1152], blocks)
    for d in range(1, 8):
        push(l_own, l_all.at[d - 1], zs.at[d - 1], zr.at[d - 1], column[d - 1]).wait_recv()
    entry = mm(mz_in[...], l_all[...].reshape(7 * 128, 128)).astype(BF16)
    for i in range(8):
        s_own[i] = (mm(px_in[i, :, 0:128], entry) + within[i]).astype(BF16)
    for d in range(1, 8):
        target = lax.rem(place + d, 8)
        copy = push(s_own.at[target], s_all.at[place], ss.at[d - 1], sr.at[d - 1], plane[d - 1])
        copy.start()
        sends.append(copy)
    s_all[place] = s_own[place]
    for d in range(1, 8):
        source = lax.rem(place + 8 - d, 8)
        push(s_own.at[0], s_all.at[source], ss.at[d - 1], sr.at[d - 1], plane[d - 1]).wait_recv()
    for e in range(HEADS):
        cols = slice(e * 128, (e + 1) * 128)
        delta = local[e] + mm(eff_in[e], s_all[e])
        norm = delta / jnp.sqrt(jnp.mean(delta * delta, axis=1, keepdims=True) + EPSILON)
        g = gate[:, cols].astype(F32)
        gated = norm * gain[...] * (g * jax.nn.sigmoid(g))
        out[:, cols] = (attn[:, cols].astype(F32) + rezero[:, cols] * gated).astype(BF16)
    for copy in sends:
        copy.wait_send()


def delta(value_in, cv, ops, attn, gate, gain, rezero):
    dma = pltpu.SemaphoreType.DMA
    vmem = pl.BlockSpec(memory_space=pltpu.VMEM)
    return pl.pallas_call(
        delta_kernel,
        out_shape=jax.ShapeDtypeStruct((ROWS, 1024), BF16),
        in_specs=[vmem] * 11,
        out_specs=vmem,
        scratch_shapes=[
            pltpu.VMEM((16, 1024), BF16),
            pltpu.VMEM((16 + ROWS, 1024), F32),
            pltpu.VMEM((ROWS, 1024), BF16),
            pltpu.VMEM((8, 128, 128), BF16),
            pltpu.VMEM((8, 128, 128), BF16),
            pltpu.VMEM((8, ROWS, 128), F32),
            pltpu.VMEM((128, 128), BF16),
            pltpu.VMEM((7, 128, 128), BF16),
            pltpu.VMEM((8, 128, 128), F32),
            pltpu.VMEM((8, 128, 128), BF16),
            pltpu.VMEM((8, 128, 128), BF16),
            dma((1,)),
            dma((1,)),
            dma((7,)),
            dma((7,)),
            dma((7,)),
            dma((7,)),
            dma((7,)),
            dma((7,)),
        ],
        compiler_params=pltpu.CompilerParams(collective_id=3, has_side_effects=True),
        name="delta_rule",
    )(value_in, cv, *ops, attn, gate, gain, rezero)


def body(
    queries,
    attention_keys,
    attention_values,
    attn_gate,
    segment_ids,
    value_proj,
    linear_queries,
    linear_keys,
    conv_queries,
    conv_keys,
    conv_values,
    decay_logits,
    beta_logits,
    decay_base,
    decay_bias,
    output_gate,
    output_gain,
    rezero_gate,
):
    ctx = lax.axis_index("ctx")
    seg_tile = jnp.pad(segment_ids, (0, 1024 - ROWS), constant_values=127).reshape(8, 128)
    kv, segs = window(attention_keys, attention_values, seg_tile)
    back = 16 - jnp.arange(WINDOW, dtype=jnp.int32)
    source = ctx - back + 64
    step = source // 8
    step = (ctx + 64) // 8 - step
    y_hi, x = (source // 4) % 2, source % 4
    missing = jnp.maximum(16 - ctx, 0).astype(jnp.int32).reshape(1)
    slots = jnp.concatenate(
        [step * 8 + y_hi * 4 + x, x * 6 + step * 2 + y_hi, missing]
    ).astype(jnp.int32)
    seg_query = jnp.tile(segment_ids, 4).reshape(1, 4 * ROWS)
    attn_out = attention(
        slots, kv.reshape(24, ROWS, 512), segs.reshape(24, 8, 128), seg_query, queries, attn_gate
    )
    everything = all_heads(attn_out)
    squares = jnp.mean(jnp.square(everything.astype(F32)), axis=1, keepdims=True)
    summed = jnp.dot(everything, value_proj, preferred_element_type=F32)
    value_in = (summed / jnp.sqrt(squares + EPSILON)).astype(BF16)
    log_decay = -jnp.exp(decay_base)[:, None] * jax.nn.softplus(
        decay_logits.T + decay_bias[:, None]
    )
    beta = jax.nn.sigmoid(beta_logits.T)
    ops = linear(
        linear_queries,
        linear_keys,
        conv_queries.astype(F32),
        conv_keys.astype(F32),
        log_decay,
        beta,
    )
    return delta(
        value_in,
        conv_values.astype(F32),
        ops,
        attn_out,
        output_gate,
        output_gain.reshape(1, 128),
        rezero_gate.reshape(1, 1024),
    )


def solution(mesh):
    placed = (
        P("ctx", "head"),
        P("ctx", None),
        P("ctx", None),
        P("ctx", "head"),
        P("ctx"),
        P(None, "head"),
        P("ctx", "head"),
        P("ctx", "head"),
        P(None, "head"),
        P(None, "head"),
        P(None, "head"),
        P("ctx", "head"),
        P("ctx", "head"),
        P("head"),
        P("head"),
        P("ctx", "head"),
        P(),
        P("head"),
    )
    return jax.shard_map(
        body, mesh=mesh, in_specs=placed, out_specs=P("ctx", "head"), check_vma=False
    )
```

```python
import functools

import jax
import jax.numpy as jnp
from jax import lax
from jax.experimental import pallas as pl
from jax.experimental.pallas import tpu as pltpu
from jax.sharding import PartitionSpec as P

MESH = pl.DeviceIdType.MESH
EPSILON = 1e-06
NEGATIVE = -1e30
HIGH = lax.Precision.HIGHEST
F32 = jnp.float32
BF16 = jnp.bfloat16

ROWS = 192
HALF = 96
WINDOW = 17
HEADS = 8


def coords():
    ctx = lax.axis_index("ctx")
    head = lax.axis_index("head")
    z, place = lax.div(ctx, 8), lax.rem(ctx, 8)
    y_hi, x = lax.div(place, 4), lax.rem(place, 4)
    y_lo, core = lax.div(head, 2), lax.rem(head, 2)
    return ctx, head, z, place, y_hi, x, y_lo, core


def greet(sources):
    barrier = pltpu.get_barrier_semaphore()
    for device in sources:
        pl.semaphore_signal(barrier, inc=1, device_id=device, device_id_type=MESH)
    pl.semaphore_wait(barrier, len(sources))


def push(src, dst, send_sem, recv_sem, device):
    return pltpu.make_async_remote_copy(
        src_ref=src,
        dst_ref=dst,
        send_sem=send_sem,
        recv_sem=recv_sem,
        device_id=device,
        device_id_type=MESH,
    )


def window_sources():
    ctx, head, z, place, y_hi, x, y_lo, core = coords()
    partner = (ctx, y_lo * 2 + 1 - core)
    across = (z * 8 + (1 - y_hi) * 4 + x, (1 - y_lo) * 2 + core)
    below = (lax.rem(z + 7, 8) * 8 + place, head)
    beside = [(z * 8 + y_hi * 4 + lax.rem(x + d, 4), head) for d in (1, 3, 2)]
    return [partner, across, below] + beside


def window_steps(
    keys, values, seg, kv, segs, own, own_seg, load_sem, y_s, y_r, z_s, z_r, x_s, x_r, f_s, f_r
):
    ctx, head, z, place, y_hi, x, y_lo, core = coords()
    partner = (ctx, y_lo * 2 + 1 - core)
    across = (z * 8 + (1 - y_hi) * 4 + x, (1 - y_lo) * 2 + core)
    above = (lax.rem(z + 1, 8) * 8 + place, head)
    beside = [(z * 8 + y_hi * 4 + lax.rem(x + d, 4), head) for d in (1, 3, 2)]
    rows = pl.ds(pl.multiple_of(core * HALF, 16), HALF)
    mine = pl.ds(pl.multiple_of(y_lo * 256, 256), 256)
    other = pl.ds(pl.multiple_of((1 - y_lo) * 256, 256), 256)

    local = [
        pltpu.make_async_copy(keys.at[:, mine], own.at[0, :, pl.ds(0, 256)], load_sem.at[0]),
        pltpu.make_async_copy(values.at[:, mine], own.at[0, :, pl.ds(256, 256)], load_sem.at[1]),
        pltpu.make_async_copy(keys.at[rows, other], own.at[1, rows, pl.ds(0, 256)], load_sem.at[2]),
        pltpu.make_async_copy(
            values.at[rows, other], own.at[1, rows, pl.ds(256, 256)], load_sem.at[3]
        ),
        pltpu.make_async_copy(seg, own_seg, load_sem.at[4]),
    ]
    for copy in local:
        copy.start()
    yield
    for copy in local:
        copy.wait()
    keep = [
        pltpu.make_async_copy(own.at[0], kv.at[0, y_hi, x], load_sem.at[5]),
        pltpu.make_async_copy(own_seg, segs.at[x, 0, y_hi], load_sem.at[6]),
    ]
    for copy in keep:
        copy.start()

    y_copy = [
        push(own.at[1, rows], kv.at[0, y_hi, x, rows], y_s.at[0], y_r.at[0], across),
        push(own_seg, segs.at[x, 0, y_hi], y_s.at[1], y_r.at[1], across),
    ]
    for copy in y_copy:
        copy.start()
    y_back = [
        push(own.at[1, rows], kv.at[0, 1 - y_hi, x, rows], y_s.at[0], y_r.at[0], across),
        push(own_seg, segs.at[x, 0, 1 - y_hi], y_s.at[1], y_r.at[1], across),
    ]

    def z_push(step, yh, index):
        return push(
            kv.at[step, yh, x, rows], kv.at[step + 1, yh, x, rows], z_s.at[index], z_r.at[index], above
        )

    def forward(step, yh, xs, index):
        return push(
            kv.at[step, yh, xs, rows], kv.at[step, yh, xs, rows], f_s.at[index], f_r.at[index], partner
        )

    def forwarded(step, yh, xs, index):
        back = pl.ds(pl.multiple_of((1 - core) * HALF, 16), HALF)
        return push(
            kv.at[step, yh, xs, back], kv.at[step, yh, xs, back], f_s.at[index], f_r.at[index], partner
        )

    z_first = push(own.at[0, rows], kv.at[1, y_hi, x, rows], z_s.at[0], z_r.at[0], above)
    z_first.start()

    def x_push(k, step, yh, index, src=None):
        source = kv.at[step, yh, x, rows] if src is None else src
        return push(source, kv.at[step, yh, x, rows], x_s.at[k, index], x_r.at[k, index], beside[k])

    def later(k, yh):
        dest = y_hi * 4 + lax.rem(x + (1, 3, 2)[k], 4)
        return yh * 4 + x < dest

    for k in range(3):
        early = later(k, y_hi)

        @pl.when(early)
        def _(k=k):
            x_push(k, 0, y_hi, 0, own.at[0, rows]).start()

    yield
    for copy in y_back:
        copy.wait_recv()
    z_second = z_push(0, 1 - y_hi, 1)
    z_second.start()
    z_seg = push(segs.at[x, 0], segs.at[x, 1], z_s.at[4], z_r.at[4], above)
    keep[1].wait()
    z_seg.start()
    for k in range(3):
        early = later(k, 1 - y_hi)

        @pl.when(early)
        def _(k=k):
            x_push(k, 0, 1 - y_hi, 1).start()

    forwards = [(0, 1 - y_hi, x)]
    forward(*forwards[0], 0).start()

    yield
    for yh, index in ((y_hi, 0), (1 - y_hi, 1)):
        z_push(0, yh, index).wait_recv()
        z_push(1, yh, 2 + index).start()
        for k in range(3):
            x_push(k, 1, yh, 2 + index).start()
        forward(1, yh, x, len(forwards)).start()
        forwards.append((1, yh, x))
    yield
    z_seg.wait_recv()
    z_seg_on = push(segs.at[x, 1], segs.at[x, 2], z_s.at[5], z_r.at[5], above)
    z_seg_on.start()
    for yh, index in ((y_hi, 0), (1 - y_hi, 1)):
        z_push(1, yh, 2 + index).wait_recv()
        for k in range(3):
            late = jnp.logical_not(later(k, yh))

            @pl.when(late)
            def _(k=k, yh=yh, index=index):
                x_push(k, 2, yh, index).start()

        forward(2, yh, x, len(forwards)).start()
        forwards.append((2, yh, x))
    yield
    z_seg_on.wait_recv()
    x_seg = [
        push(segs.at[x], segs.at[x], x_s.at[k, 4], x_r.at[k, 4], beside[k]) for k in range(3)
    ]
    for copy in x_seg:
        copy.start()

    def came(k, step, yh, index):
        xs = lax.rem(x + (3, 1, 2)[k], 4)
        return push(
            kv.at[step, yh, xs, rows], kv.at[step, yh, xs, rows], x_s.at[k, index], x_r.at[k, index], beside[k]
        )

    def choice(k, yh):
        xs = lax.rem(x + (3, 1, 2)[k], 4)
        return jnp.where(yh * 4 + xs < place, 0, 2)

    yield
    for k in range(3):
        xs = lax.rem(x + (3, 1, 2)[k], 4)
        for yh, index in ((y_hi, 0), (1 - y_hi, 1)):
            came(k, 1, yh, 2 + index).wait_recv()
            forward(1, yh, xs, len(forwards)).start()
            forwards.append((1, yh, xs))
    yield
    for k in range(3):
        xs = lax.rem(x + (3, 1, 2)[k], 4)
        for yh, index in ((y_hi, 0), (1 - y_hi, 1)):
            step = choice(k, yh)
            came(k, step, yh, index).wait_recv()
            forward(step, yh, xs, len(forwards)).start()
            forwards.append((step, yh, xs))
        x_seg_in = push(segs.at[xs], segs.at[xs], x_s.at[k, 4], x_r.at[k, 4], beside[k])
        x_seg_in.wait_recv()
    yield
    for index, where in enumerate(forwards):
        forwarded(*where, index).wait_recv()
    keep[0].wait()
    for copy in y_copy:
        copy.wait_send()
    z_first.wait_send()
    z_second.wait_send()
    z_seg.wait_send()
    z_seg_on.wait_send()
    for index in (2, 3):
        z_push(1, y_hi, index).wait_send()
    for k in range(3):
        for index in range(4):
            x_push(k, 1, y_hi, index).wait_send()
        x_seg[k].wait_send()
    for index, where in enumerate(forwards):
        forward(*where, index).wait_send()


def attention_kernel(slots, kv, segs, seg_query, queries, gate, out, q_all, first, m_sc, l_sc, acc):
    step = pl.program_id(0)
    lanes = 4 * ROWS

    @pl.when(step == 0)
    def _():
        for h in range(4):
            q_all[h * ROWS : (h + 1) * ROWS, :] = (
                queries[:, h * 256 : (h + 1) * 256].astype(F32) * 0.0625
            ).astype(BF16)
        m_sc[...] = jnp.full(m_sc.shape, NEGATIVE, F32)
        l_sc[...] = jnp.zeros(l_sc.shape, F32)
        acc[...] = jnp.zeros(acc.shape, F32)
        begin = jnp.zeros((1, lanes), jnp.int32)
        missing = slots[2 * WINDOW]
        for doc in range(8):
            less = jnp.zeros((8, 128), jnp.int32)
            for b in range(WINDOW):
                block = segs[slots[WINDOW + b]]
                less = less + jnp.where((block < doc) & (b >= missing), 1, 0)
            total = jnp.sum(less) + missing * ROWS
            begin = jnp.where(seg_query[...] == doc, total, begin)
        first[...] = jnp.broadcast_to(begin, first.shape)

    block = lax.rem(WINDOW - 1 + step, WINDOW)
    keys, values = kv[0, :, 0:256], kv[0, :, 256:512]
    scores = lax.dot_general(
        keys, q_all[...], (((1,), (1,)), ((), ())), preferred_element_type=F32
    )
    key_pos = block * ROWS + lax.broadcasted_iota(jnp.int32, (ROWS, lanes), 0)
    token = lax.broadcasted_iota(jnp.int32, (1, lanes), 1)
    for h in range(1, 4):
        token = jnp.where(token >= ROWS, token - ROWS, token)
    last = (WINDOW - 1) * ROWS + token
    allowed = (key_pos >= first[0:1, :]) & (key_pos <= last)
    scores = jnp.where(allowed, scores, NEGATIVE)
    m_old = m_sc[0:1, :]
    m_new = jnp.maximum(m_old, jnp.max(scores, axis=0, keepdims=True))
    scale = jnp.exp(m_old - m_new)
    weights = jnp.exp(scores - m_new)
    l_sc[0:1, :] = l_sc[0:1, :] * scale + jnp.sum(weights, axis=0, keepdims=True)
    m_sc[0:1, :] = m_new
    added = lax.dot_general(
        values, weights.astype(BF16), (((0,), (0,)), ((), ())), preferred_element_type=F32
    )
    acc[...] = acc[...] * scale + added

    @pl.when(step == WINDOW - 1)
    def _():
        mean = jnp.transpose(acc[...] / l_sc[0:1, :])
        for h in range(4):
            g = gate[:, h * 256 : (h + 1) * 256].astype(F32)
            out[:, h * 256 : (h + 1) * 256] = (
                jax.nn.sigmoid(g) * mean[h * ROWS : (h + 1) * ROWS, :]
            ).astype(BF16)


def attention(slots, kv, segs, seg_query, queries, gate):
    full = lambda shape: pl.BlockSpec(shape, lambda s, slots: (0,) * len(shape))
    lanes = 4 * ROWS
    return pl.pallas_call(
        attention_kernel,
        out_shape=jax.ShapeDtypeStruct((ROWS, 1024), BF16),
        grid_spec=pltpu.PrefetchScalarGridSpec(
            num_scalar_prefetch=1,
            grid=(WINDOW,),
            in_specs=[
                pl.BlockSpec(
                    (1, ROWS, 512),
                    lambda s, slots: (slots[lax.rem(WINDOW - 1 + s, WINDOW)], 0, 0),
                ),
                full((24, 8, 128)),
                full((1, lanes)),
                full((ROWS, 1024)),
                full((ROWS, 1024)),
            ],
            out_specs=full((ROWS, 1024)),
            scratch_shapes=[
                pltpu.VMEM((lanes, 256), BF16),
                pltpu.VMEM((8, lanes), jnp.int32),
                pltpu.VMEM((8, lanes), F32),
                pltpu.VMEM((8, lanes), F32),
                pltpu.VMEM((256, lanes), F32),
            ],
        ),
        name="window_attention",
    )(slots, kv, segs, seg_query, queries, gate)


PIECES = 3


def heads_kernel(own, out, l_sem, p_s, p_r, a_s, a_r, f_s, f_r):
    ctx, head, z, place, y_hi, x, y_lo, core = coords()
    partner = (ctx, y_lo * 2 + 1 - core)
    across = (ctx, (1 - y_lo) * 2 + core)
    greet([partner, across])
    size = ROWS // PIECES

    def part(i, h):
        return out.at[pl.ds(i * size, size), pl.ds(pl.multiple_of(h * 1024, 1024), 1024)]

    def piece(i):
        return own.at[pl.ds(i * size, size)]

    far, farther = (1 - y_lo) * 2 + core, (1 - y_lo) * 2 + 1 - core
    keep = [pltpu.make_async_copy(piece(i), part(i, head), l_sem.at[i]) for i in range(PIECES)]
    for i in range(PIECES):
        push(piece(i), part(i, head), a_s.at[i], a_r.at[i], across).start()
        push(piece(i), part(i, head), p_s.at[i], p_r.at[i], partner).start()
        keep[i].start()
    for i in range(PIECES):
        push(piece(i), part(i, far), a_s.at[i], a_r.at[i], across).wait_recv()
        push(part(i, far), part(i, far), f_s.at[i], f_r.at[i], partner).start()
    for i in range(PIECES):
        near = y_lo * 2 + 1 - core
        push(piece(i), part(i, near), p_s.at[i], p_r.at[i], partner).wait()
        push(part(i, far), part(i, farther), f_s.at[i], f_r.at[i], partner).wait()
        push(piece(i), part(i, far), a_s.at[i], a_r.at[i], across).wait_send()
        keep[i].wait()


def all_heads(own):
    dma = pltpu.SemaphoreType.DMA
    return pl.pallas_call(
        heads_kernel,
        out_shape=jax.ShapeDtypeStruct((ROWS, 4096), BF16),
        in_specs=[pl.BlockSpec(memory_space=pltpu.VMEM)],
        out_specs=pl.BlockSpec(memory_space=pl.ANY),
        scratch_shapes=[dma((PIECES,))] * 7,
        compiler_params=pltpu.CompilerParams(collective_id=1, has_side_effects=True),
        name="all_heads",
    )(own)


def mm(a, b, precision=None):
    return jnp.dot(a, b, precision=precision, preferred_element_type=F32)


def mm_t(a, b, precision=None):
    return lax.dot_general(
        a, b, (((1,), (1,)), ((), ())), precision=precision, preferred_element_type=F32
    )


def split(x):
    high = x.astype(BF16)
    return high, (x - high.astype(F32)).astype(BF16)


def mm_split(a, b, product=mm):
    (ah, al), (bh, bl) = a, b
    return product(ah, bh) + (product(ah, bl) + product(al, bh))


def mm_low(a, b):
    return mm(a.astype(BF16), b.astype(BF16))


def causal(ext, taps, width):
    total = jnp.zeros((ROWS, width), F32)
    for m in range(4):
        total = total + taps[m : m + 1, :] * ext[13 + m : 13 + m + ROWS, 0:width]
    return total / (1.0 + jnp.exp(-total))


def triangle(size, strict):
    row = lax.broadcasted_iota(jnp.int32, (size, size), 0)
    col = lax.broadcasted_iota(jnp.int32, (size, size), 1)
    return (col < row) if strict else (col <= row)


def inverse_lower(systems):
    row = lax.broadcasted_iota(jnp.int32, (ROWS, ROWS), 0)
    col = lax.broadcasted_iota(jnp.int32, (ROWS, ROWS), 1)
    unit = jnp.where(row == col, 1.0, 0.0)
    block = lax.div(row, 8) == lax.div(col, 8)
    powers = [jnp.where(block, -m, 0.0) for m in systems]
    inverses = [unit + p for p in powers]
    for _ in range(2):
        powers = [mm_low(p, p) for p in powers]
        inverses = [x + mm_low(x, p) for x, p in zip(inverses, powers)]
    size = 8
    while size < ROWS:
        pair = 2 * size
        below = (lax.div(row, pair) == lax.div(col, pair)) & (lax.div(row, size) != lax.div(col, size))
        if pair >= ROWS:
            below = lax.div(row, size) != lax.div(col, size)
        lows = [x.astype(BF16) for x in inverses]
        inner = [
            mm(jnp.where(below, m, 0.0).astype(BF16), x) for m, x in zip(systems, lows)
        ]
        inverses = [
            x - mm(low, i.astype(BF16)) for x, low, i in zip(inverses, lows, inner)
        ]
        size = pair
        yield None
    splits = [split(x) for x in inverses]
    rests = [
        (unit - x) - mm_split(split(m), xs) for m, x, xs in zip(systems, inverses, splits)
    ]
    yield [x + mm(xs[0], r.astype(BF16)) for x, xs, r in zip(inverses, splits, rests)]


def linear_kernel(
    lq, lk, cq, ck, decay, beta, keys, values, seg,
    h_out, eff_out, g_out, px_out, mz_out, kv, segs,
    own, own_seg, w_load, wy_s, wy_r, wz_s, wz_r, wx_s, wx_r, wf_s, wf_r,
    halo, ext, q_sc, k_sc, t_own, t_all, row_sc, p_own, p_all,
    hs, hr, ts, tr, zs, zr,
):
    ctx, head, z, place, y_hi, x, y_lo, core = coords()
    following = (lax.rem(ctx + 1, 64), head)
    previous = (lax.rem(ctx + 63, 64), head)
    plane = [(z * 8 + lax.rem(place + d, 8), head) for d in range(1, 8)]
    column = [(lax.rem(z + d, 8) * 8 + place, head) for d in range(1, 8)]
    transfers = window_steps(
        keys, values, seg, kv, segs, own, own_seg, w_load,
        wy_s, wy_r, wz_s, wz_r, wx_s, wx_r, wf_s, wf_r,
    )
    next(transfers)
    greet([previous] + plane + column + window_sources())
    tail = pl.ds(ROWS - 16, 16)
    edge = [
        push(lq.at[tail], halo.at[0], hs.at[0], hr.at[0], following),
        push(lk.at[tail], halo.at[1], hs.at[1], hr.at[1], following),
    ]
    for copy in edge:
        copy.start()
    next(transfers)
    for copy in edge:
        copy.wait()
    begins = ctx == 0
    for source, taps, index, target in ((lq, cq, 0, q_sc), (lk, ck, 1, k_sc)):
        ext[0:16, :] = jnp.where(begins, 0.0, halo[index].astype(F32))
        ext[16 : 16 + ROWS, :] = source[...].astype(F32)
        conv = causal(ext, taps, 512)
        for n in range(4):
            part = conv[:, n * 128 : (n + 1) * 128]
            part = part / jnp.sqrt(jnp.sum(part * part, axis=1, keepdims=True) + EPSILON)
            if index == 0:
                part = part * (1.0 / 128.0**0.5)
            target[n] = part
        next(transfers)
    lower = triangle(ROWS, False)
    strict = triangle(ROWS, True)
    ones = jnp.where(lower, 1.0, 0.0)
    row = lax.broadcasted_iota(jnp.int32, (ROWS, ROWS), 0)
    col = lax.broadcasted_iota(jnp.int32, (ROWS, ROWS), 1)
    unit = jnp.where(row == col, 1.0, 0.0)
    unit_k = jnp.where(
        lax.broadcasted_iota(jnp.int32, (128, 128), 0)
        == lax.broadcasted_iota(jnp.int32, (128, 128), 1),
        1.0,
        0.0,
    )
    sum_row = mm_t(decay[...], ones, HIGH)
    sum_col = mm_t(ones, decay[...], HIGH)
    beta_col = mm_t(unit, beta[...], HIGH)
    group = 2
    for base in range(0, HEADS, group):
        parts, systems = [], []
        for e in range(base, base + group):
            q, k = q_sc[e // 2], k_sc[e // 2]
            if e % 2 == 0:
                k_split = split(k)
                key_key = mm_split(k_split, k_split, mm_t)
                query_key = mm_split(split(q), k_split, mm_t)
            c_col, c_row = sum_col[:, e : e + 1], sum_row[e : e + 1, :]
            b_col, b_row = beta_col[:, e : e + 1], beta[e : e + 1, :]
            fade = jnp.exp(jnp.where(lower, c_col - c_row, NEGATIVE))
            systems.append(jnp.where(strict, b_col * key_key * fade, 0.0))
            parts.append((q, k, c_col, b_col, b_row, query_key * fade))
        for inverses in inverse_lower(systems):
            pass
        for e, inverse, (q, k, c_col, b_col, b_row, scores) in zip(
            range(base, base + group), inverses, parts
        ):
            grown = jnp.exp(c_col)
            inverse = split(inverse)
            scores = split(scores)
            weight_keys = split(mm_split(inverse, split((b_col * grown) * k)))
            eff_out[e] = (grown * q - mm_split(scores, weight_keys)).astype(BF16)
            h_out[e] = (mm_split(scores, inverse) * b_row).astype(BF16)
            final = c_col[ROWS - 1 : ROWS, :]
            decayed = split(jnp.transpose(jnp.exp(final - c_col) * k))
            t_own[e] = (jnp.exp(final) * unit_k - mm_split(decayed, weight_keys)).astype(BF16)
            g_out[e] = (mm_split(decayed, inverse) * b_row).astype(BF16)
        next(transfers, None)

    sends = []
    for d in range(1, 8):
        owner = lax.rem(place + d, 8)
        copy = push(t_own.at[owner], t_all.at[8 - d], ts.at[d - 1], tr.at[7 - d], plane[d - 1])
        copy.start()
        sends.append(copy)
    t_all[0] = t_own[place]
    for d in range(1, 8):
        push(t_own.at[0], t_all.at[8 - d], ts.at[d - 1], tr.at[7 - d], plane[d - 1]).wait_recv()
    row_sc[...] = jnp.zeros(row_sc.shape, F32)
    row_sc[:, 0:128] = unit_k
    px_out[0] = row_sc[...].astype(BF16)
    for i in range(8):
        current = t_all[lax.rem(i - place + 8, 8)]
        width = (i + 1) * 128
        high, low = split(row_sc[:, 0:width])
        row_sc[:, 0:width] = mm(current, high) + mm(current, low)
        row_sc[:, width : width + 128] = unit_k
        px_out[i + 1] = row_sc[...].astype(BF16)
    p_own[...] = row_sc[:, 0:128].astype(BF16)
    for d in range(1, 8):
        copy = push(p_own, p_all.at[d - 1], zs.at[d - 1], zr.at[d - 1], column[d - 1])
        copy.start()
        sends.append(copy)
    for d in range(1, 8):
        push(p_own, p_all.at[d - 1], zs.at[d - 1], zr.at[d - 1], column[d - 1]).wait_recv()
    running = unit_k
    for r in range(1, 8):
        valid = z >= r
        mz_out[:, (r - 1) * 128 : r * 128] = jnp.where(valid, running, 0.0).astype(BF16)
        if r < 7:
            high, low = split(running)
            running = mm(high, p_all[r - 1]) + mm(low, p_all[r - 1])
    for copy in sends:
        copy.wait_send()
    for _ in transfers:
        pass


def linear(lq, lk, cq, ck, decay, beta, keys, values, seg_tile):
    dma = pltpu.SemaphoreType.DMA
    vmem = pl.BlockSpec(memory_space=pltpu.VMEM)
    anywhere = pl.BlockSpec(memory_space=pl.ANY)
    return pl.pallas_call(
        linear_kernel,
        out_shape=(
            jax.ShapeDtypeStruct((HEADS, ROWS, ROWS), BF16),
            jax.ShapeDtypeStruct((HEADS, ROWS, 128), BF16),
            jax.ShapeDtypeStruct((HEADS, 128, ROWS), BF16),
            jax.ShapeDtypeStruct((9, 128, 1152), BF16),
            jax.ShapeDtypeStruct((128, 896), BF16),
            jax.ShapeDtypeStruct((3, 2, 4, ROWS, 512), BF16),
            jax.ShapeDtypeStruct((4, 3, 2, 8, 128), jnp.int32),
        ),
        in_specs=[vmem] * 6 + [anywhere] * 3,
        out_specs=[vmem] * 5 + [anywhere] * 2,
        scratch_shapes=[
            pltpu.VMEM((2, ROWS, 512), BF16),
            pltpu.VMEM((8, 128), jnp.int32),
            dma((7,)),
            dma((2,)),
            dma((2,)),
            dma((6,)),
            dma((6,)),
            dma((3, 5)),
            dma((3, 5)),
            dma((17,)),
            dma((17,)),
            pltpu.VMEM((2, 16, 512), BF16),
            pltpu.VMEM((16 + ROWS, 512), F32),
            pltpu.VMEM((4, ROWS, 128), F32),
            pltpu.VMEM((4, ROWS, 128), F32),
            pltpu.VMEM((8, 128, 128), BF16),
            pltpu.VMEM((8, 128, 128), BF16),
            pltpu.VMEM((128, 1152), F32),
            pltpu.VMEM((128, 128), BF16),
            pltpu.VMEM((7, 128, 128), BF16),
            dma((2,)),
            dma((2,)),
            dma((7,)),
            dma((7,)),
            dma((7,)),
            dma((7,)),
        ],
        compiler_params=pltpu.CompilerParams(collective_id=2, has_side_effects=True),
        name="linear_operators",
    )(lq, lk, cq, ck, decay, beta, keys, values, seg_tile)


def delta_kernel(
    value_in, cv, h_in, eff_in, g_in, px_in, mz_in, attn, gate, gain, rezero, out,
    halo, ext, v_sc, b_own, b_all, local, l_own, l_all, within, s_own, s_all,
    hs, hr, bs, br, zs, zr, ss, sr,
):
    ctx, head, z, place, y_hi, x, y_lo, core = coords()
    following = (lax.rem(ctx + 1, 64), head)
    previous = (lax.rem(ctx + 63, 64), head)
    plane = [(z * 8 + lax.rem(place + d, 8), head) for d in range(1, 8)]
    column = [(lax.rem(z + d, 8) * 8 + place, head) for d in range(1, 8)]
    greet([previous] + plane + column)
    edge = push(value_in.at[pl.ds(ROWS - 16, 16)], halo, hs.at[0], hr.at[0], following)
    edge.start()
    ext[16 : 16 + ROWS, :] = value_in[...].astype(F32)
    edge.wait()
    ext[0:16, :] = jnp.where(ctx == 0, 0.0, halo[...].astype(F32))
    v_sc[...] = causal(ext, cv, 1024).astype(BF16)
    for e in range(HEADS):
        b_own[e] = mm(g_in[e], v_sc[:, e * 128 : (e + 1) * 128]).astype(BF16)
    sends = []
    for d in range(1, 8):
        owner = lax.rem(place + d, 8)
        copy = push(b_own.at[owner], b_all.at[place], bs.at[d - 1], br.at[d - 1], plane[d - 1])
        copy.start()
        sends.append(copy)
    b_all[place] = b_own[place]
    for e in range(HEADS):
        local[e] = mm(h_in[e], v_sc[:, e * 128 : (e + 1) * 128])
    for d in range(1, 8):
        source = lax.rem(place + 8 - d, 8)
        push(b_own.at[0], b_all.at[source], bs.at[d - 1], br.at[d - 1], plane[d - 1]).wait_recv()
    blocks = b_all[...].reshape(8 * 128, 128)
    l_own[...] = mm(px_in[8, :, 128:1152], blocks).astype(BF16)
    for d in range(1, 8):
        copy = push(l_own, l_all.at[d - 1], zs.at[d - 1], zr.at[d - 1], column[d - 1])
        copy.start()
        sends.append(copy)
    for i in range(8):
        within[i] = mm(px_in[i, :, 128:1152], blocks)
    for d in range(1, 8):
        push(l_own, l_all.at[d - 1], zs.at[d - 1], zr.at[d - 1], column[d - 1]).wait_recv()
    entry = mm(mz_in[...], l_all[...].reshape(7 * 128, 128)).astype(BF16)
    for i in range(8):
        s_own[i] = (mm(px_in[i, :, 0:128], entry) + within[i]).astype(BF16)
    for d in range(1, 8):
        target = lax.rem(place + d, 8)
        copy = push(s_own.at[target], s_all.at[place], ss.at[d - 1], sr.at[d - 1], plane[d - 1])
        copy.start()
        sends.append(copy)
    s_all[place] = s_own[place]
    for d in range(1, 8):
        source = lax.rem(place + 8 - d, 8)
        push(s_own.at[0], s_all.at[source], ss.at[d - 1], sr.at[d - 1], plane[d - 1]).wait_recv()
    for e in range(HEADS):
        cols = slice(e * 128, (e + 1) * 128)
        delta = local[e] + mm(eff_in[e], s_all[e])
        norm = delta / jnp.sqrt(jnp.mean(delta * delta, axis=1, keepdims=True) + EPSILON)
        g = gate[:, cols].astype(F32)
        gated = norm * gain[...] * (g * jax.nn.sigmoid(g))
        out[:, cols] = (attn[:, cols].astype(F32) + rezero[:, cols] * gated).astype(BF16)
    for copy in sends:
        copy.wait_send()


def delta(value_in, cv, ops, attn, gate, gain, rezero):
    dma = pltpu.SemaphoreType.DMA
    vmem = pl.BlockSpec(memory_space=pltpu.VMEM)
    return pl.pallas_call(
        delta_kernel,
        out_shape=jax.ShapeDtypeStruct((ROWS, 1024), BF16),
        in_specs=[vmem] * 11,
        out_specs=vmem,
        scratch_shapes=[
            pltpu.VMEM((16, 1024), BF16),
            pltpu.VMEM((16 + ROWS, 1024), F32),
            pltpu.VMEM((ROWS, 1024), BF16),
            pltpu.VMEM((8, 128, 128), BF16),
            pltpu.VMEM((8, 128, 128), BF16),
            pltpu.VMEM((8, ROWS, 128), F32),
            pltpu.VMEM((128, 128), BF16),
            pltpu.VMEM((7, 128, 128), BF16),
            pltpu.VMEM((8, 128, 128), F32),
            pltpu.VMEM((8, 128, 128), BF16),
            pltpu.VMEM((8, 128, 128), BF16),
            dma((1,)),
            dma((1,)),
            dma((7,)),
            dma((7,)),
            dma((7,)),
            dma((7,)),
            dma((7,)),
            dma((7,)),
        ],
        compiler_params=pltpu.CompilerParams(collective_id=3, has_side_effects=True),
        name="delta_rule",
    )(value_in, cv, *ops, attn, gate, gain, rezero)


def body(
    queries,
    attention_keys,
    attention_values,
    attn_gate,
    segment_ids,
    value_proj,
    linear_queries,
    linear_keys,
    conv_queries,
    conv_keys,
    conv_values,
    decay_logits,
    beta_logits,
    decay_base,
    decay_bias,
    output_gate,
    output_gain,
    rezero_gate,
):
    ctx = lax.axis_index("ctx")
    seg_tile = jnp.pad(segment_ids, (0, 1024 - ROWS), constant_values=127).reshape(8, 128)
    log_decay = -jnp.exp(decay_base)[:, None] * jax.nn.softplus(
        decay_logits.T + decay_bias[:, None]
    )
    beta = jax.nn.sigmoid(beta_logits.T)
    *ops, kv, segs = linear(
        linear_queries,
        linear_keys,
        conv_queries.astype(F32),
        conv_keys.astype(F32),
        log_decay,
        beta,
        attention_keys,
        attention_values,
        seg_tile,
    )
    back = 16 - jnp.arange(WINDOW, dtype=jnp.int32)
    source = ctx - back + 64
    step = source // 8
    step = (ctx + 64) // 8 - step
    y_hi, x = (source // 4) % 2, source % 4
    missing = jnp.maximum(16 - ctx, 0).astype(jnp.int32).reshape(1)
    slots = jnp.concatenate(
        [step * 8 + y_hi * 4 + x, x * 6 + step * 2 + y_hi, missing]
    ).astype(jnp.int32)
    seg_query = jnp.tile(segment_ids, 4).reshape(1, 4 * ROWS)
    attn_out = attention(
        slots, kv.reshape(24, ROWS, 512), segs.reshape(24, 8, 128), seg_query, queries, attn_gate
    )
    everything = all_heads(attn_out)
    squares = jnp.mean(jnp.square(everything.astype(F32)), axis=1, keepdims=True)
    summed = jnp.dot(everything, value_proj, preferred_element_type=F32)
    value_in = (summed / jnp.sqrt(squares + EPSILON)).astype(BF16)
    return delta(
        value_in,
        conv_values.astype(F32),
        ops,
        attn_out,
        output_gate,
        output_gain.reshape(1, 128),
        rezero_gate.reshape(1, 1024),
    )


def solution(mesh):
    placed = (
        P("ctx", "head"),
        P("ctx", None),
        P("ctx", None),
        P("ctx", "head"),
        P("ctx"),
        P(None, "head"),
        P("ctx", "head"),
        P("ctx", "head"),
        P(None, "head"),
        P(None, "head"),
        P(None, "head"),
        P("ctx", "head"),
        P("ctx", "head"),
        P("head"),
        P("head"),
        P("ctx", "head"),
        P(),
        P("head"),
    )
    return jax.shard_map(
        body, mesh=mesh, in_specs=placed, out_specs=P("ctx", "head"), check_vma=False
    )
```

```python
import functools

import jax
import jax.numpy as jnp
from jax import lax
from jax.experimental import pallas as pl
from jax.experimental.pallas import tpu as pltpu
from jax.sharding import PartitionSpec as P

MESH = pl.DeviceIdType.MESH
EPSILON = 1e-06
NEGATIVE = -1e30
HIGH = lax.Precision.HIGHEST
F32 = jnp.float32
BF16 = jnp.bfloat16

ROWS = 192
HALF = 96
WINDOW = 17
HEADS = 8


def coords():
    ctx = lax.axis_index("ctx")
    head = lax.axis_index("head")
    z, place = lax.div(ctx, 8), lax.rem(ctx, 8)
    y_hi, x = lax.div(place, 4), lax.rem(place, 4)
    y_lo, core = lax.div(head, 2), lax.rem(head, 2)
    return ctx, head, z, place, y_hi, x, y_lo, core


def greet(sources):
    barrier = pltpu.get_barrier_semaphore()
    for device in sources:
        pl.semaphore_signal(barrier, inc=1, device_id=device, device_id_type=MESH)
    pl.semaphore_wait(barrier, len(sources))


def push(src, dst, send_sem, recv_sem, device):
    return pltpu.make_async_remote_copy(
        src_ref=src,
        dst_ref=dst,
        send_sem=send_sem,
        recv_sem=recv_sem,
        device_id=device,
        device_id_type=MESH,
    )


def window_sources():
    ctx, head, z, place, y_hi, x, y_lo, core = coords()
    partner = (ctx, y_lo * 2 + 1 - core)
    across = (z * 8 + (1 - y_hi) * 4 + x, (1 - y_lo) * 2 + core)
    below = (lax.rem(z + 7, 8) * 8 + place, head)
    beside = [(z * 8 + y_hi * 4 + lax.rem(x + d, 4), head) for d in (1, 3, 2)]
    return [partner, across, below] + beside


def window_steps(
    keys, values, seg, kv, segs, own, own_seg, load_sem, y_s, y_r, z_s, z_r, x_s, x_r, f_s, f_r
):
    ctx, head, z, place, y_hi, x, y_lo, core = coords()
    partner = (ctx, y_lo * 2 + 1 - core)
    across = (z * 8 + (1 - y_hi) * 4 + x, (1 - y_lo) * 2 + core)
    above = (lax.rem(z + 1, 8) * 8 + place, head)
    beside = [(z * 8 + y_hi * 4 + lax.rem(x + d, 4), head) for d in (1, 3, 2)]
    rows = pl.ds(pl.multiple_of(core * HALF, 16), HALF)
    mine = pl.ds(pl.multiple_of(y_lo * 256, 256), 256)
    other = pl.ds(pl.multiple_of((1 - y_lo) * 256, 256), 256)

    local = [
        pltpu.make_async_copy(keys.at[:, mine], own.at[0, :, pl.ds(0, 256)], load_sem.at[0]),
        pltpu.make_async_copy(values.at[:, mine], own.at[0, :, pl.ds(256, 256)], load_sem.at[1]),
        pltpu.make_async_copy(keys.at[rows, other], own.at[1, rows, pl.ds(0, 256)], load_sem.at[2]),
        pltpu.make_async_copy(
            values.at[rows, other], own.at[1, rows, pl.ds(256, 256)], load_sem.at[3]
        ),
        pltpu.make_async_copy(seg, own_seg, load_sem.at[4]),
    ]
    for copy in local:
        copy.start()
    yield
    for copy in local:
        copy.wait()
    keep = [
        pltpu.make_async_copy(own.at[0], kv.at[0, y_hi, x], load_sem.at[5]),
        pltpu.make_async_copy(own_seg, segs.at[x, 0, y_hi], load_sem.at[6]),
    ]
    for copy in keep:
        copy.start()

    y_copy = [
        push(own.at[1, rows], kv.at[0, y_hi, x, rows], y_s.at[0], y_r.at[0], across),
        push(own_seg, segs.at[x, 0, y_hi], y_s.at[1], y_r.at[1], across),
    ]
    for copy in y_copy:
        copy.start()
    y_back = [
        push(own.at[1, rows], kv.at[0, 1 - y_hi, x, rows], y_s.at[0], y_r.at[0], across),
        push(own_seg, segs.at[x, 0, 1 - y_hi], y_s.at[1], y_r.at[1], across),
    ]

    def z_push(step, yh, index):
        return push(
            kv.at[step, yh, x, rows], kv.at[step + 1, yh, x, rows], z_s.at[index], z_r.at[index], above
        )

    def forward(step, yh, xs, index):
        return push(
            kv.at[step, yh, xs, rows], kv.at[step, yh, xs, rows], f_s.at[index], f_r.at[index], partner
        )

    def forwarded(step, yh, xs, index):
        back = pl.ds(pl.multiple_of((1 - core) * HALF, 16), HALF)
        return push(
            kv.at[step, yh, xs, back], kv.at[step, yh, xs, back], f_s.at[index], f_r.at[index], partner
        )

    z_first = push(own.at[0, rows], kv.at[1, y_hi, x, rows], z_s.at[0], z_r.at[0], above)
    z_first.start()

    def x_push(k, step, yh, index, src=None):
        source = kv.at[step, yh, x, rows] if src is None else src
        return push(source, kv.at[step, yh, x, rows], x_s.at[k, index], x_r.at[k, index], beside[k])

    def later(k, yh):
        dest = y_hi * 4 + lax.rem(x + (1, 3, 2)[k], 4)
        return yh * 4 + x < dest

    for k in range(3):
        early = later(k, y_hi)

        @pl.when(early)
        def _(k=k):
            x_push(k, 0, y_hi, 0, own.at[0, rows]).start()

    yield
    for copy in y_back:
        copy.wait_recv()
    z_second = z_push(0, 1 - y_hi, 1)
    z_second.start()
    z_seg = push(segs.at[x, 0], segs.at[x, 1], z_s.at[4], z_r.at[4], above)
    keep[1].wait()
    z_seg.start()
    for k in range(3):
        early = later(k, 1 - y_hi)

        @pl.when(early)
        def _(k=k):
            x_push(k, 0, 1 - y_hi, 1).start()

    forwards = [(0, 1 - y_hi, x)]
    forward(*forwards[0], 0).start()

    yield
    for yh, index in ((y_hi, 0), (1 - y_hi, 1)):
        z_push(0, yh, index).wait_recv()
        z_push(1, yh, 2 + index).start()
        for k in range(3):
            x_push(k, 1, yh, 2 + index).start()
        forward(1, yh, x, len(forwards)).start()
        forwards.append((1, yh, x))
    yield
    z_seg.wait_recv()
    z_seg_on = push(segs.at[x, 1], segs.at[x, 2], z_s.at[5], z_r.at[5], above)
    z_seg_on.start()
    for yh, index in ((y_hi, 0), (1 - y_hi, 1)):
        z_push(1, yh, 2 + index).wait_recv()
        for k in range(3):
            late = jnp.logical_not(later(k, yh))

            @pl.when(late)
            def _(k=k, yh=yh, index=index):
                x_push(k, 2, yh, index).start()

        forward(2, yh, x, len(forwards)).start()
        forwards.append((2, yh, x))
    yield
    z_seg_on.wait_recv()
    x_seg = [
        push(segs.at[x], segs.at[x], x_s.at[k, 4], x_r.at[k, 4], beside[k]) for k in range(3)
    ]
    for copy in x_seg:
        copy.start()

    def came(k, step, yh, index):
        xs = lax.rem(x + (3, 1, 2)[k], 4)
        return push(
            kv.at[step, yh, xs, rows], kv.at[step, yh, xs, rows], x_s.at[k, index], x_r.at[k, index], beside[k]
        )

    def choice(k, yh):
        xs = lax.rem(x + (3, 1, 2)[k], 4)
        return jnp.where(yh * 4 + xs < place, 0, 2)

    yield
    for k in range(3):
        xs = lax.rem(x + (3, 1, 2)[k], 4)
        for yh, index in ((y_hi, 0), (1 - y_hi, 1)):
            came(k, 1, yh, 2 + index).wait_recv()
            forward(1, yh, xs, len(forwards)).start()
            forwards.append((1, yh, xs))
    yield
    for k in range(3):
        xs = lax.rem(x + (3, 1, 2)[k], 4)
        for yh, index in ((y_hi, 0), (1 - y_hi, 1)):
            step = choice(k, yh)
            came(k, step, yh, index).wait_recv()
            forward(step, yh, xs, len(forwards)).start()
            forwards.append((step, yh, xs))
        x_seg_in = push(segs.at[xs], segs.at[xs], x_s.at[k, 4], x_r.at[k, 4], beside[k])
        x_seg_in.wait_recv()
    yield
    for index, where in enumerate(forwards):
        forwarded(*where, index).wait_recv()
    keep[0].wait()
    for copy in y_copy:
        copy.wait_send()
    z_first.wait_send()
    z_second.wait_send()
    z_seg.wait_send()
    z_seg_on.wait_send()
    for index in (2, 3):
        z_push(1, y_hi, index).wait_send()
    for k in range(3):
        for index in range(4):
            x_push(k, 1, y_hi, index).wait_send()
        x_seg[k].wait_send()
    for index, where in enumerate(forwards):
        forward(*where, index).wait_send()


def attention_kernel(slots, kv, segs, seg_query, queries, gate, out, q_all, first, m_sc, l_sc, acc):
    step = pl.program_id(0)
    lanes = 4 * ROWS

    @pl.when(step == 0)
    def _():
        for h in range(4):
            q_all[h * ROWS : (h + 1) * ROWS, :] = (
                queries[:, h * 256 : (h + 1) * 256].astype(F32) * 0.0625
            ).astype(BF16)
        m_sc[...] = jnp.full(m_sc.shape, NEGATIVE, F32)
        l_sc[...] = jnp.zeros(l_sc.shape, F32)
        acc[...] = jnp.zeros(acc.shape, F32)
        begin = jnp.zeros((1, lanes), jnp.int32)
        missing = slots[2 * WINDOW]
        for doc in range(8):
            less = jnp.zeros((8, 128), jnp.int32)
            for b in range(WINDOW):
                block = segs[slots[WINDOW + b]]
                less = less + jnp.where((block < doc) & (b >= missing), 1, 0)
            total = jnp.sum(less) + missing * ROWS
            begin = jnp.where(seg_query[...] == doc, total, begin)
        first[...] = jnp.broadcast_to(begin, first.shape)

    block = lax.rem(WINDOW - 1 + step, WINDOW)
    keys, values = kv[0, :, 0:256], kv[0, :, 256:512]
    scores = lax.dot_general(
        keys, q_all[...], (((1,), (1,)), ((), ())), preferred_element_type=F32
    )
    key_pos = block * ROWS + lax.broadcasted_iota(jnp.int32, (ROWS, lanes), 0)
    token = lax.broadcasted_iota(jnp.int32, (1, lanes), 1)
    for h in range(1, 4):
        token = jnp.where(token >= ROWS, token - ROWS, token)
    last = (WINDOW - 1) * ROWS + token
    allowed = (key_pos >= first[0:1, :]) & (key_pos <= last)
    scores = jnp.where(allowed, scores, NEGATIVE)
    m_old = m_sc[0:1, :]
    m_new = jnp.maximum(m_old, jnp.max(scores, axis=0, keepdims=True))
    scale = jnp.exp(m_old - m_new)
    weights = jnp.exp(scores - m_new)
    l_sc[0:1, :] = l_sc[0:1, :] * scale + jnp.sum(weights, axis=0, keepdims=True)
    m_sc[0:1, :] = m_new
    added = lax.dot_general(
        values, weights.astype(BF16), (((0,), (0,)), ((), ())), preferred_element_type=F32
    )
    acc[...] = acc[...] * scale + added

    @pl.when(step == WINDOW - 1)
    def _():
        mean = jnp.transpose(acc[...] / l_sc[0:1, :])
        for h in range(4):
            g = gate[:, h * 256 : (h + 1) * 256].astype(F32)
            out[:, h * 256 : (h + 1) * 256] = (
                jax.nn.sigmoid(g) * mean[h * ROWS : (h + 1) * ROWS, :]
            ).astype(BF16)


def attention(slots, kv, segs, seg_query, queries, gate):
    full = lambda shape: pl.BlockSpec(shape, lambda s, slots: (0,) * len(shape))
    lanes = 4 * ROWS
    return pl.pallas_call(
        attention_kernel,
        out_shape=jax.ShapeDtypeStruct((ROWS, 1024), BF16),
        grid_spec=pltpu.PrefetchScalarGridSpec(
            num_scalar_prefetch=1,
            grid=(WINDOW,),
            in_specs=[
                pl.BlockSpec(
                    (1, ROWS, 512),
                    lambda s, slots: (slots[lax.rem(WINDOW - 1 + s, WINDOW)], 0, 0),
                ),
                full((24, 8, 128)),
                full((1, lanes)),
                full((ROWS, 1024)),
                full((ROWS, 1024)),
            ],
            out_specs=full((ROWS, 1024)),
            scratch_shapes=[
                pltpu.VMEM((lanes, 256), BF16),
                pltpu.VMEM((8, lanes), jnp.int32),
                pltpu.VMEM((8, lanes), F32),
                pltpu.VMEM((8, lanes), F32),
                pltpu.VMEM((256, lanes), F32),
            ],
        ),
        name="window_attention",
    )(slots, kv, segs, seg_query, queries, gate)


def mm(a, b, precision=None):
    return jnp.dot(a, b, precision=precision, preferred_element_type=F32)


def mm_t(a, b, precision=None):
    return lax.dot_general(
        a, b, (((1,), (1,)), ((), ())), precision=precision, preferred_element_type=F32
    )


def split(x):
    high = x.astype(BF16)
    return high, (x - high.astype(F32)).astype(BF16)


def mm_split(a, b, product=mm):
    (ah, al), (bh, bl) = a, b
    return product(ah, bh) + (product(ah, bl) + product(al, bh))


def mm_low(a, b):
    return mm(a.astype(BF16), b.astype(BF16))


PIECES = 3


def heads_kernel(
    own, t_own, out, px_out, mz_out, t_all, row_sc, p_own, p_all,
    l_sem, p_s, p_r, a_s, a_r, f_s, f_r, ts, tr, zs, zr,
):
    ctx, head, z, place, y_hi, x, y_lo, core = coords()
    partner = (ctx, y_lo * 2 + 1 - core)
    across = (ctx, (1 - y_lo) * 2 + core)
    plane = [(z * 8 + lax.rem(place + d, 8), head) for d in range(1, 8)]
    column = [(lax.rem(z + d, 8) * 8 + place, head) for d in range(1, 8)]
    greet([partner, across] + plane + column)
    size = ROWS // PIECES

    def part(i, h):
        return out.at[pl.ds(i * size, size), pl.ds(pl.multiple_of(h * 1024, 1024), 1024)]

    def piece(i):
        return own.at[pl.ds(i * size, size)]

    far, farther = (1 - y_lo) * 2 + core, (1 - y_lo) * 2 + 1 - core
    sends = []
    for d in range(1, 8):
        owner = lax.rem(place + d, 8)
        copy = push(t_own.at[owner], t_all.at[8 - d], ts.at[d - 1], tr.at[7 - d], plane[d - 1])
        copy.start()
        sends.append(copy)
    keep = [pltpu.make_async_copy(piece(i), part(i, head), l_sem.at[i]) for i in range(PIECES)]
    for i in range(PIECES):
        push(piece(i), part(i, head), a_s.at[i], a_r.at[i], across).start()
        push(piece(i), part(i, head), p_s.at[i], p_r.at[i], partner).start()
        keep[i].start()

    def pass_on(i):
        push(piece(i), part(i, far), a_s.at[i], a_r.at[i], across).wait_recv()
        push(part(i, far), part(i, far), f_s.at[i], f_r.at[i], partner).start()

    unit_k = jnp.where(
        lax.broadcasted_iota(jnp.int32, (128, 128), 0)
        == lax.broadcasted_iota(jnp.int32, (128, 128), 1),
        1.0,
        0.0,
    )
    t_all[0] = t_own[place]
    row_sc[...] = jnp.zeros(row_sc.shape, F32)
    row_sc[:, 0:128] = unit_k
    px_out[0] = row_sc[...].astype(BF16)
    for d in range(1, 8):
        push(t_own.at[0], t_all.at[8 - d], ts.at[d - 1], tr.at[7 - d], plane[d - 1]).wait_recv()
    pass_on(0)
    for i in range(8):
        current = t_all[lax.rem(i - place + 8, 8)]
        width = (i + 1) * 128
        high, low = split(row_sc[:, 0:width])
        row_sc[:, 0:width] = mm(current, high) + mm(current, low)
        row_sc[:, width : width + 128] = unit_k
        px_out[i + 1] = row_sc[...].astype(BF16)
        if i == 4:
            pass_on(1)
    p_own[...] = row_sc[:, 0:128].astype(BF16)
    for d in range(1, 8):
        copy = push(p_own, p_all.at[d - 1], zs.at[d - 1], zr.at[d - 1], column[d - 1])
        copy.start()
        sends.append(copy)
    pass_on(2)
    for d in range(1, 8):
        push(p_own, p_all.at[d - 1], zs.at[d - 1], zr.at[d - 1], column[d - 1]).wait_recv()
    running = unit_k
    for r in range(1, 8):
        valid = z >= r
        mz_out[:, (r - 1) * 128 : r * 128] = jnp.where(valid, running, 0.0).astype(BF16)
        if r < 7:
            high, low = split(running)
            running = mm(high, p_all[r - 1]) + mm(low, p_all[r - 1])
    for i in range(PIECES):
        near = y_lo * 2 + 1 - core
        push(piece(i), part(i, near), p_s.at[i], p_r.at[i], partner).wait()
        push(part(i, far), part(i, farther), f_s.at[i], f_r.at[i], partner).wait()
        push(piece(i), part(i, far), a_s.at[i], a_r.at[i], across).wait_send()
        keep[i].wait()
    for copy in sends:
        copy.wait_send()


def all_heads(own, transitions):
    dma = pltpu.SemaphoreType.DMA
    vmem = pl.BlockSpec(memory_space=pltpu.VMEM)
    return pl.pallas_call(
        heads_kernel,
        out_shape=(
            jax.ShapeDtypeStruct((ROWS, 4096), BF16),
            jax.ShapeDtypeStruct((9, 128, 1152), BF16),
            jax.ShapeDtypeStruct((128, 896), BF16),
        ),
        in_specs=[vmem] * 2,
        out_specs=[pl.BlockSpec(memory_space=pl.ANY), vmem, vmem],
        scratch_shapes=[
            pltpu.VMEM((8, 128, 128), BF16),
            pltpu.VMEM((128, 1152), F32),
            pltpu.VMEM((128, 128), BF16),
            pltpu.VMEM((7, 128, 128), BF16),
        ]
        + [dma((PIECES,))] * 7
        + [dma((7,))] * 4,
        compiler_params=pltpu.CompilerParams(collective_id=1, has_side_effects=True),
        name="all_heads",
    )(own, transitions)


def causal(ext, taps, width):
    total = jnp.zeros((ROWS, width), F32)
    taps = taps[...].astype(F32)
    for m in range(4):
        total = total + taps[m : m + 1, :] * ext[13 + m : 13 + m + ROWS, 0:width]
    return total / (1.0 + jnp.exp(-total))


def triangle(size, strict):
    row = lax.broadcasted_iota(jnp.int32, (size, size), 0)
    col = lax.broadcasted_iota(jnp.int32, (size, size), 1)
    return (col < row) if strict else (col <= row)


def inverse_lower(systems):
    row = lax.broadcasted_iota(jnp.int32, (ROWS, ROWS), 0)
    col = lax.broadcasted_iota(jnp.int32, (ROWS, ROWS), 1)
    unit = jnp.where(row == col, 1.0, 0.0)
    block = lax.div(row, 8) == lax.div(col, 8)
    powers = [jnp.where(block, -m, 0.0) for m in systems]
    inverses = [unit + p for p in powers]
    for _ in range(2):
        powers = [mm_low(p, p) for p in powers]
        inverses = [x + mm_low(x, p) for x, p in zip(inverses, powers)]
    size = 8
    while size < ROWS:
        pair = 2 * size
        below = (lax.div(row, pair) == lax.div(col, pair)) & (lax.div(row, size) != lax.div(col, size))
        if pair >= ROWS:
            below = lax.div(row, size) != lax.div(col, size)
        lows = [x.astype(BF16) for x in inverses]
        inner = [
            mm(jnp.where(below, m, 0.0).astype(BF16), x) for m, x in zip(systems, lows)
        ]
        inverses = [
            x - mm(low, i.astype(BF16)) for x, low, i in zip(inverses, lows, inner)
        ]
        size = pair
        yield None
    splits = [split(x) for x in inverses]
    rests = [
        (unit - x) - mm_split(split(m), xs) for m, x, xs in zip(systems, inverses, splits)
    ]
    yield [x + mm(xs[0], r.astype(BF16)) for x, xs, r in zip(inverses, splits, rests)]


def linear_kernel(
    lq, lk, cq, ck, decay_logits, beta_logits, decay_base, decay_bias, keys, values, seg,
    h_out, eff_out, g_out, t_own, kv, segs,
    own, own_seg, w_load, wy_s, wy_r, wz_s, wz_r, wx_s, wx_r, wf_s, wf_r,
    halo, ext, q_sc, k_sc, row_sc, hs, hr,
):
    ctx, head, z, place, y_hi, x, y_lo, core = coords()
    following = (lax.rem(ctx + 1, 64), head)
    previous = (lax.rem(ctx + 63, 64), head)
    transfers = window_steps(
        keys, values, seg, kv, segs, own, own_seg, w_load,
        wy_s, wy_r, wz_s, wz_r, wx_s, wx_r, wf_s, wf_r,
    )
    next(transfers)
    greet([previous] + window_sources())
    tail = pl.ds(ROWS - 16, 16)
    edge = [
        push(lq.at[tail], halo.at[0], hs.at[0], hr.at[0], following),
        push(lk.at[tail], halo.at[1], hs.at[1], hr.at[1], following),
    ]
    for copy in edge:
        copy.start()
    next(transfers)
    for copy in edge:
        copy.wait()
    begins = ctx == 0
    for source, taps, index, target in ((lq, cq, 0, q_sc), (lk, ck, 1, k_sc)):
        ext[0:16, :] = jnp.where(begins, 0.0, halo[index].astype(F32))
        ext[16 : 16 + ROWS, :] = source[...].astype(F32)
        conv = causal(ext, taps, 512)
        for n in range(4):
            part = conv[:, n * 128 : (n + 1) * 128]
            part = part / jnp.sqrt(jnp.sum(part * part, axis=1, keepdims=True) + EPSILON)
            if index == 0:
                part = part * (1.0 / 128.0**0.5)
            target[n] = part
        next(transfers)
    lower = triangle(ROWS, False)
    strict = triangle(ROWS, True)
    ones = jnp.where(lower, 1.0, 0.0)
    row = lax.broadcasted_iota(jnp.int32, (ROWS, ROWS), 0)
    col = lax.broadcasted_iota(jnp.int32, (ROWS, ROWS), 1)
    unit = jnp.where(row == col, 1.0, 0.0)
    unit_k = jnp.where(
        lax.broadcasted_iota(jnp.int32, (128, 128), 0)
        == lax.broadcasted_iota(jnp.int32, (128, 128), 1),
        1.0,
        0.0,
    )
    shifted = decay_logits[...] + decay_bias[...]
    softplus = jnp.maximum(shifted, 0.0) + jnp.log1p(jnp.exp(-jnp.abs(shifted)))
    decay = -jnp.exp(decay_base[...]) * softplus
    beta_col = jax.nn.sigmoid(beta_logits[...])
    onward = jnp.where(row <= col, 1.0, 0.0)
    sum_col = mm(ones, decay, HIGH)
    across_rows = (((0,), (0,)), ((), ()))
    row_sc[0] = lax.dot_general(
        decay, onward, across_rows, precision=HIGH, preferred_element_type=F32
    )
    row_sc[1] = lax.dot_general(
        beta_col, unit, across_rows, precision=HIGH, preferred_element_type=F32
    )
    group = 2
    for base in range(0, HEADS, group):
        parts, systems = [], []
        for e in range(base, base + group):
            q, k = q_sc[e // 2], k_sc[e // 2]
            if e % 2 == 0:
                k_split = split(k)
                key_key = mm_split(k_split, k_split, mm_t)
                query_key = mm_split(split(q), k_split, mm_t)
            c_col, c_row = sum_col[:, e : e + 1], row_sc[0, e : e + 1, :]
            b_col, b_row = beta_col[:, e : e + 1], row_sc[1, e : e + 1, :]
            fade = jnp.exp(jnp.where(lower, c_col - c_row, NEGATIVE))
            systems.append(jnp.where(strict, b_col * key_key * fade, 0.0))
            parts.append((q, k, c_col, b_col, b_row, query_key * fade))
        for inverses in inverse_lower(systems):
            pass
        for e, inverse, (q, k, c_col, b_col, b_row, scores) in zip(
            range(base, base + group), inverses, parts
        ):
            grown = jnp.exp(c_col)
            inverse = split(inverse)
            scores = split(scores)
            weight_keys = split(mm_split(inverse, split((b_col * grown) * k)))
            eff_out[e] = (grown * q - mm_split(scores, weight_keys)).astype(BF16)
            h_out[e] = (mm_split(scores, inverse) * b_row).astype(BF16)
            final = c_col[ROWS - 1 : ROWS, :]
            decayed = split(jnp.transpose(jnp.exp(final - c_col) * k))
            t_own[e] = (jnp.exp(final) * unit_k - mm_split(decayed, weight_keys)).astype(BF16)
            g_out[e] = (mm_split(decayed, inverse) * b_row).astype(BF16)
        next(transfers, None)
    for _ in transfers:
        pass


def linear(*operands):
    dma = pltpu.SemaphoreType.DMA
    vmem = pl.BlockSpec(memory_space=pltpu.VMEM)
    anywhere = pl.BlockSpec(memory_space=pl.ANY)
    return pl.pallas_call(
        linear_kernel,
        out_shape=(
            jax.ShapeDtypeStruct((HEADS, ROWS, ROWS), BF16),
            jax.ShapeDtypeStruct((HEADS, ROWS, 128), BF16),
            jax.ShapeDtypeStruct((HEADS, 128, ROWS), BF16),
            jax.ShapeDtypeStruct((HEADS, 128, 128), BF16),
            jax.ShapeDtypeStruct((3, 2, 4, ROWS, 512), BF16),
            jax.ShapeDtypeStruct((4, 3, 2, 8, 128), jnp.int32),
        ),
        in_specs=[vmem] * 8 + [anywhere] * 3,
        out_specs=[vmem] * 4 + [anywhere] * 2,
        scratch_shapes=[
            pltpu.VMEM((2, ROWS, 512), BF16),
            pltpu.VMEM((8, 128), jnp.int32),
            dma((7,)),
            dma((2,)),
            dma((2,)),
            dma((6,)),
            dma((6,)),
            dma((3, 5)),
            dma((3, 5)),
            dma((17,)),
            dma((17,)),
            pltpu.VMEM((2, 16, 512), BF16),
            pltpu.VMEM((16 + ROWS, 512), F32),
            pltpu.VMEM((4, ROWS, 128), F32),
            pltpu.VMEM((4, ROWS, 128), F32),
            pltpu.VMEM((2, HEADS, ROWS), F32),
            dma((2,)),
            dma((2,)),
        ],
        compiler_params=pltpu.CompilerParams(collective_id=2, has_side_effects=True),
        name="linear_operators",
    )(*operands)


def delta_kernel(
    value_in, cv, h_in, eff_in, g_in, px_in, mz_in, attn, gate, gain, rezero, out,
    halo, ext, v_sc, b_own, b_all, local, gated_sc, l_own, l_all, within, s_own, s_all,
    hs, hr, bs, br, zs, zr, ss, sr,
):
    ctx, head, z, place, y_hi, x, y_lo, core = coords()
    following = (lax.rem(ctx + 1, 64), head)
    previous = (lax.rem(ctx + 63, 64), head)
    plane = [(z * 8 + lax.rem(place + d, 8), head) for d in range(1, 8)]
    column = [(lax.rem(z + d, 8) * 8 + place, head) for d in range(1, 8)]
    greet([previous] + plane + column)
    edge = push(value_in.at[pl.ds(ROWS - 16, 16)], halo, hs.at[0], hr.at[0], following)
    edge.start()
    ext[16 : 16 + ROWS, :] = value_in[...].astype(F32)
    edge.wait()
    ext[0:16, :] = jnp.where(ctx == 0, 0.0, halo[...].astype(F32))
    v_sc[...] = causal(ext, cv, 1024).astype(BF16)
    for e in range(HEADS):
        b_own[e] = mm(g_in[e], v_sc[:, e * 128 : (e + 1) * 128]).astype(BF16)
    sends = []
    for d in range(1, 8):
        owner = lax.rem(place + d, 8)
        copy = push(b_own.at[owner], b_all.at[place], bs.at[d - 1], br.at[d - 1], plane[d - 1])
        copy.start()
        sends.append(copy)
    b_all[place] = b_own[place]
    for e in range(HEADS):
        local[e] = mm(h_in[e], v_sc[:, e * 128 : (e + 1) * 128])
    for d in range(1, 8):
        source = lax.rem(place + 8 - d, 8)
        push(b_own.at[0], b_all.at[source], bs.at[d - 1], br.at[d - 1], plane[d - 1]).wait_recv()
    blocks = b_all[...].reshape(8 * 128, 128)
    l_own[...] = mm(px_in[8, :, 128:1152], blocks).astype(BF16)
    for d in range(1, 8):
        copy = push(l_own, l_all.at[d - 1], zs.at[d - 1], zr.at[d - 1], column[d - 1])
        copy.start()
        sends.append(copy)
    for i in range(8):
        within[i] = mm(px_in[i, :, 128:1152], blocks)
    for e in range(HEADS):
        cols = slice(e * 128, (e + 1) * 128)
        g = gate[:, cols].astype(F32)
        gated_sc[e] = rezero[:, cols] * gain[...] * (g * jax.nn.sigmoid(g))
    for d in range(1, 8):
        push(l_own, l_all.at[d - 1], zs.at[d - 1], zr.at[d - 1], column[d - 1]).wait_recv()
    entry = mm(mz_in[...], l_all[...].reshape(7 * 128, 128)).astype(BF16)
    for i in range(8):
        s_own[i] = (mm(px_in[i, :, 0:128], entry) + within[i]).astype(BF16)
    for d in range(1, 8):
        target = lax.rem(place + d, 8)
        copy = push(s_own.at[target], s_all.at[place], ss.at[d - 1], sr.at[d - 1], plane[d - 1])
        copy.start()
        sends.append(copy)
    s_all[place] = s_own[place]
    for d in range(1, 8):
        source = lax.rem(place + 8 - d, 8)
        push(s_own.at[0], s_all.at[source], ss.at[d - 1], sr.at[d - 1], plane[d - 1]).wait_recv()
    for e in range(HEADS):
        cols = slice(e * 128, (e + 1) * 128)
        delta = local[e] + mm(eff_in[e], s_all[e])
        norm = delta / jnp.sqrt(jnp.mean(delta * delta, axis=1, keepdims=True) + EPSILON)
        out[:, cols] = (attn[:, cols].astype(F32) + norm * gated_sc[e]).astype(BF16)
    for copy in sends:
        copy.wait_send()


def delta(value_in, cv, ops, attn, gate, gain, rezero):
    dma = pltpu.SemaphoreType.DMA
    vmem = pl.BlockSpec(memory_space=pltpu.VMEM)
    return pl.pallas_call(
        delta_kernel,
        out_shape=jax.ShapeDtypeStruct((ROWS, 1024), BF16),
        in_specs=[vmem] * 11,
        out_specs=vmem,
        scratch_shapes=[
            pltpu.VMEM((16, 1024), BF16),
            pltpu.VMEM((16 + ROWS, 1024), F32),
            pltpu.VMEM((ROWS, 1024), BF16),
            pltpu.VMEM((8, 128, 128), BF16),
            pltpu.VMEM((8, 128, 128), BF16),
            pltpu.VMEM((8, ROWS, 128), F32),
            pltpu.VMEM((8, ROWS, 128), F32),
            pltpu.VMEM((128, 128), BF16),
            pltpu.VMEM((7, 128, 128), BF16),
            pltpu.VMEM((8, 128, 128), F32),
            pltpu.VMEM((8, 128, 128), BF16),
            pltpu.VMEM((8, 128, 128), BF16),
            dma((1,)),
            dma((1,)),
            dma((7,)),
            dma((7,)),
            dma((7,)),
            dma((7,)),
            dma((7,)),
            dma((7,)),
        ],
        compiler_params=pltpu.CompilerParams(collective_id=3, has_side_effects=True),
        name="delta_rule",
    )(value_in, cv, *ops, attn, gate, gain, rezero)


def body(
    queries,
    attention_keys,
    attention_values,
    attn_gate,
    segment_ids,
    value_proj,
    linear_queries,
    linear_keys,
    conv_queries,
    conv_keys,
    conv_values,
    decay_logits,
    beta_logits,
    decay_base,
    decay_bias,
    output_gate,
    output_gain,
    rezero_gate,
):
    ctx = lax.axis_index("ctx")
    seg_tile = jnp.pad(segment_ids, (0, 1024 - ROWS), constant_values=127).reshape(8, 128)
    *ops, transitions, kv, segs = linear(
        linear_queries,
        linear_keys,
        conv_queries,
        conv_keys,
        decay_logits,
        beta_logits,
        decay_base.reshape(1, HEADS),
        decay_bias.reshape(1, HEADS),
        attention_keys,
        attention_values,
        seg_tile,
    )
    back = 16 - jnp.arange(WINDOW, dtype=jnp.int32)
    source = ctx - back + 64
    step = source // 8
    step = (ctx + 64) // 8 - step
    y_hi, x = (source // 4) % 2, source % 4
    missing = jnp.maximum(16 - ctx, 0).astype(jnp.int32).reshape(1)
    slots = jnp.concatenate(
        [step * 8 + y_hi * 4 + x, x * 6 + step * 2 + y_hi, missing]
    ).astype(jnp.int32)
    seg_query = jnp.tile(segment_ids, 4).reshape(1, 4 * ROWS)
    attn_out = attention(
        slots, kv.reshape(24, ROWS, 512), segs.reshape(24, 8, 128), seg_query, queries, attn_gate
    )
    everything, px, mz = all_heads(attn_out, transitions)
    squares = jnp.mean(jnp.square(everything.astype(F32)), axis=1, keepdims=True)
    summed = jnp.dot(everything, value_proj, preferred_element_type=F32)
    value_in = (summed / jnp.sqrt(squares + EPSILON)).astype(BF16)
    return delta(
        value_in,
        conv_values,
        (*ops, px, mz),
        attn_out,
        output_gate,
        output_gain.reshape(1, 128),
        rezero_gate.reshape(1, 1024),
    )


def solution(mesh):
    placed = (
        P("ctx", "head"),
        P("ctx", None),
        P("ctx", None),
        P("ctx", "head"),
        P("ctx"),
        P(None, "head"),
        P("ctx", "head"),
        P("ctx", "head"),
        P(None, "head"),
        P(None, "head"),
        P(None, "head"),
        P("ctx", "head"),
        P("ctx", "head"),
        P("head"),
        P("head"),
        P("ctx", "head"),
        P(),
        P("head"),
    )
    return jax.shard_map(
        body, mesh=mesh, in_specs=placed, out_specs=P("ctx", "head"), check_vma=False
    )
```

```python
import functools

import jax
import jax.numpy as jnp
from jax import lax
from jax.experimental import pallas as pl
from jax.experimental.pallas import tpu as pltpu
from jax.sharding import PartitionSpec as P

MESH = pl.DeviceIdType.MESH
EPSILON = 1e-06
NEGATIVE = -1e30
HIGH = lax.Precision.HIGHEST
F32 = jnp.float32
BF16 = jnp.bfloat16

ROWS = 192
HALF = 96
WINDOW = 17
HEADS = 8


def coords():
    ctx = lax.axis_index("ctx")
    head = lax.axis_index("head")
    z, place = lax.div(ctx, 8), lax.rem(ctx, 8)
    y_hi, x = lax.div(place, 4), lax.rem(place, 4)
    y_lo, core = lax.div(head, 2), lax.rem(head, 2)
    return ctx, head, z, place, y_hi, x, y_lo, core


def greet(sources):
    barrier = pltpu.get_barrier_semaphore()
    for device in sources:
        pl.semaphore_signal(barrier, inc=1, device_id=device, device_id_type=MESH)
    pl.semaphore_wait(barrier, len(sources))


def push(src, dst, send_sem, recv_sem, device):
    return pltpu.make_async_remote_copy(
        src_ref=src,
        dst_ref=dst,
        send_sem=send_sem,
        recv_sem=recv_sem,
        device_id=device,
        device_id_type=MESH,
    )


def window_sources():
    ctx, head, z, place, y_hi, x, y_lo, core = coords()
    partner = (ctx, y_lo * 2 + 1 - core)
    across = (z * 8 + (1 - y_hi) * 4 + x, (1 - y_lo) * 2 + core)
    below = (lax.rem(z + 7, 8) * 8 + place, head)
    beside = [(z * 8 + y_hi * 4 + lax.rem(x + d, 4), head) for d in (1, 3, 2)]
    return [partner, across, below] + beside


def window_steps(
    keys, values, seg, kv, segs, own, own_seg, load_sem, y_s, y_r, z_s, z_r, x_s, x_r, f_s, f_r
):
    ctx, head, z, place, y_hi, x, y_lo, core = coords()
    partner = (ctx, y_lo * 2 + 1 - core)
    across = (z * 8 + (1 - y_hi) * 4 + x, (1 - y_lo) * 2 + core)
    above = (lax.rem(z + 1, 8) * 8 + place, head)
    beside = [(z * 8 + y_hi * 4 + lax.rem(x + d, 4), head) for d in (1, 3, 2)]
    rows = pl.ds(pl.multiple_of(core * HALF, 16), HALF)
    mine = pl.ds(pl.multiple_of(y_lo * 256, 256), 256)
    other = pl.ds(pl.multiple_of((1 - y_lo) * 256, 256), 256)

    local = [
        pltpu.make_async_copy(keys.at[:, mine], own.at[0, :, pl.ds(0, 256)], load_sem.at[0]),
        pltpu.make_async_copy(values.at[:, mine], own.at[0, :, pl.ds(256, 256)], load_sem.at[1]),
        pltpu.make_async_copy(keys.at[rows, other], own.at[1, rows, pl.ds(0, 256)], load_sem.at[2]),
        pltpu.make_async_copy(
            values.at[rows, other], own.at[1, rows, pl.ds(256, 256)], load_sem.at[3]
        ),
        pltpu.make_async_copy(seg, own_seg, load_sem.at[4]),
    ]
    for copy in local:
        copy.start()
    yield
    for copy in local:
        copy.wait()
    keep = [
        pltpu.make_async_copy(own.at[0], kv.at[0, y_hi, x], load_sem.at[5]),
        pltpu.make_async_copy(own_seg, segs.at[x, 0, y_hi], load_sem.at[6]),
    ]
    for copy in keep:
        copy.start()

    y_copy = [
        push(own.at[1, rows], kv.at[0, y_hi, x, rows], y_s.at[0], y_r.at[0], across),
        push(own_seg, segs.at[x, 0, y_hi], y_s.at[1], y_r.at[1], across),
    ]
    for copy in y_copy:
        copy.start()
    y_back = [
        push(own.at[1, rows], kv.at[0, 1 - y_hi, x, rows], y_s.at[0], y_r.at[0], across),
        push(own_seg, segs.at[x, 0, 1 - y_hi], y_s.at[1], y_r.at[1], across),
    ]

    def z_push(step, yh, index):
        return push(
            kv.at[step, yh, x, rows], kv.at[step + 1, yh, x, rows], z_s.at[index], z_r.at[index], above
        )

    def forward(step, yh, xs, index):
        return push(
            kv.at[step, yh, xs, rows], kv.at[step, yh, xs, rows], f_s.at[index], f_r.at[index], partner
        )

    def forwarded(step, yh, xs, index):
        back = pl.ds(pl.multiple_of((1 - core) * HALF, 16), HALF)
        return push(
            kv.at[step, yh, xs, back], kv.at[step, yh, xs, back], f_s.at[index], f_r.at[index], partner
        )

    z_first = push(own.at[0, rows], kv.at[1, y_hi, x, rows], z_s.at[0], z_r.at[0], above)
    z_first.start()

    def x_push(k, step, yh, index, src=None):
        source = kv.at[step, yh, x, rows] if src is None else src
        return push(source, kv.at[step, yh, x, rows], x_s.at[k, index], x_r.at[k, index], beside[k])

    def later(k, yh):
        dest = y_hi * 4 + lax.rem(x + (1, 3, 2)[k], 4)
        return yh * 4 + x < dest

    for k in range(3):
        early = later(k, y_hi)

        @pl.when(early)
        def _(k=k):
            x_push(k, 0, y_hi, 0, own.at[0, rows]).start()

    yield
    for copy in y_back:
        copy.wait_recv()
    z_second = z_push(0, 1 - y_hi, 1)
    z_second.start()
    z_seg = push(segs.at[x, 0], segs.at[x, 1], z_s.at[4], z_r.at[4], above)
    keep[1].wait()
    z_seg.start()
    for k in range(3):
        early = later(k, 1 - y_hi)

        @pl.when(early)
        def _(k=k):
            x_push(k, 0, 1 - y_hi, 1).start()

    forwards = [(0, 1 - y_hi, x)]
    forward(*forwards[0], 0).start()

    yield
    for yh, index in ((y_hi, 0), (1 - y_hi, 1)):
        z_push(0, yh, index).wait_recv()
        z_push(1, yh, 2 + index).start()
        for k in range(3):
            x_push(k, 1, yh, 2 + index).start()
        forward(1, yh, x, len(forwards)).start()
        forwards.append((1, yh, x))
    yield
    z_seg.wait_recv()
    z_seg_on = push(segs.at[x, 1], segs.at[x, 2], z_s.at[5], z_r.at[5], above)
    z_seg_on.start()
    for yh, index in ((y_hi, 0), (1 - y_hi, 1)):
        z_push(1, yh, 2 + index).wait_recv()
        for k in range(3):
            late = jnp.logical_not(later(k, yh))

            @pl.when(late)
            def _(k=k, yh=yh, index=index):
                x_push(k, 2, yh, index).start()

        forward(2, yh, x, len(forwards)).start()
        forwards.append((2, yh, x))
    yield
    z_seg_on.wait_recv()
    x_seg = [
        push(segs.at[x], segs.at[x], x_s.at[k, 4], x_r.at[k, 4], beside[k]) for k in range(3)
    ]
    for copy in x_seg:
        copy.start()

    def came(k, step, yh, index):
        xs = lax.rem(x + (3, 1, 2)[k], 4)
        return push(
            kv.at[step, yh, xs, rows], kv.at[step, yh, xs, rows], x_s.at[k, index], x_r.at[k, index], beside[k]
        )

    def choice(k, yh):
        xs = lax.rem(x + (3, 1, 2)[k], 4)
        return jnp.where(yh * 4 + xs < place, 0, 2)

    yield
    for k in range(3):
        xs = lax.rem(x + (3, 1, 2)[k], 4)
        for yh, index in ((y_hi, 0), (1 - y_hi, 1)):
            came(k, 1, yh, 2 + index).wait_recv()
            forward(1, yh, xs, len(forwards)).start()
            forwards.append((1, yh, xs))
    yield
    for k in range(3):
        xs = lax.rem(x + (3, 1, 2)[k], 4)
        for yh, index in ((y_hi, 0), (1 - y_hi, 1)):
            step = choice(k, yh)
            came(k, step, yh, index).wait_recv()
            forward(step, yh, xs, len(forwards)).start()
            forwards.append((step, yh, xs))
        x_seg_in = push(segs.at[xs], segs.at[xs], x_s.at[k, 4], x_r.at[k, 4], beside[k])
        x_seg_in.wait_recv()
    yield
    for index, where in enumerate(forwards):
        forwarded(*where, index).wait_recv()
    keep[0].wait()
    for copy in y_copy:
        copy.wait_send()
    z_first.wait_send()
    z_second.wait_send()
    z_seg.wait_send()
    z_seg_on.wait_send()
    for index in (2, 3):
        z_push(1, y_hi, index).wait_send()
    for k in range(3):
        for index in range(4):
            x_push(k, 1, y_hi, index).wait_send()
        x_seg[k].wait_send()
    for index, where in enumerate(forwards):
        forward(*where, index).wait_send()


def attention_kernel(slots, kv, segs, seg_query, queries, gate, out, q_all, first, m_sc, l_sc, acc):
    step = pl.program_id(0)
    lanes = 4 * ROWS

    @pl.when(step == 0)
    def _():
        for h in range(4):
            q_all[h * ROWS : (h + 1) * ROWS, :] = (
                queries[:, h * 256 : (h + 1) * 256].astype(F32) * 0.0625
            ).astype(BF16)
        m_sc[...] = jnp.full(m_sc.shape, NEGATIVE, F32)
        l_sc[...] = jnp.zeros(l_sc.shape, F32)
        acc[...] = jnp.zeros(acc.shape, F32)
        begin = jnp.zeros((1, lanes), jnp.int32)
        missing = slots[2 * WINDOW]
        for doc in range(8):
            less = jnp.zeros((8, 128), jnp.int32)
            for b in range(WINDOW):
                block = segs[slots[WINDOW + b]]
                less = less + jnp.where((block < doc) & (b >= missing), 1, 0)
            total = jnp.sum(less) + missing * ROWS
            begin = jnp.where(seg_query[...] == doc, total, begin)
        first[...] = jnp.broadcast_to(begin, first.shape)

    block = lax.rem(WINDOW - 1 + step, WINDOW)
    keys, values = kv[0, :, 0:256], kv[0, :, 256:512]
    scores = lax.dot_general(
        keys, q_all[...], (((1,), (1,)), ((), ())), preferred_element_type=F32
    )
    key_pos = block * ROWS + lax.broadcasted_iota(jnp.int32, (ROWS, lanes), 0)
    token = lax.broadcasted_iota(jnp.int32, (1, lanes), 1)
    for h in range(1, 4):
        token = jnp.where(token >= ROWS, token - ROWS, token)
    last = (WINDOW - 1) * ROWS + token
    allowed = (key_pos >= first[0:1, :]) & (key_pos <= last)
    scores = jnp.where(allowed, scores, NEGATIVE)
    m_old = m_sc[0:1, :]
    m_new = jnp.maximum(m_old, jnp.max(scores, axis=0, keepdims=True))
    scale = jnp.exp(m_old - m_new)
    weights = jnp.exp(scores - m_new)
    l_sc[0:1, :] = l_sc[0:1, :] * scale + jnp.sum(weights, axis=0, keepdims=True)
    m_sc[0:1, :] = m_new
    added = lax.dot_general(
        values, weights.astype(BF16), (((0,), (0,)), ((), ())), preferred_element_type=F32
    )
    acc[...] = acc[...] * scale + added

    @pl.when(step == WINDOW - 1)
    def _():
        mean = jnp.transpose(acc[...] / l_sc[0:1, :])
        for h in range(4):
            g = gate[:, h * 256 : (h + 1) * 256].astype(F32)
            out[:, h * 256 : (h + 1) * 256] = (
                jax.nn.sigmoid(g) * mean[h * ROWS : (h + 1) * ROWS, :]
            ).astype(BF16)


def attention(slots, kv, segs, seg_query, queries, gate):
    full = lambda shape: pl.BlockSpec(shape, lambda s, slots: (0,) * len(shape))
    lanes = 4 * ROWS
    return pl.pallas_call(
        attention_kernel,
        out_shape=jax.ShapeDtypeStruct((ROWS, 1024), BF16),
        grid_spec=pltpu.PrefetchScalarGridSpec(
            num_scalar_prefetch=1,
            grid=(WINDOW,),
            in_specs=[
                pl.BlockSpec(
                    (1, ROWS, 512),
                    lambda s, slots: (slots[lax.rem(WINDOW - 1 + s, WINDOW)], 0, 0),
                ),
                full((24, 8, 128)),
                full((1, lanes)),
                full((ROWS, 1024)),
                full((ROWS, 1024)),
            ],
            out_specs=full((ROWS, 1024)),
            scratch_shapes=[
                pltpu.VMEM((lanes, 256), BF16),
                pltpu.VMEM((8, lanes), jnp.int32),
                pltpu.VMEM((8, lanes), F32),
                pltpu.VMEM((8, lanes), F32),
                pltpu.VMEM((256, lanes), F32),
            ],
        ),
        name="window_attention",
    )(slots, kv, segs, seg_query, queries, gate)


def mm(a, b, precision=None):
    return jnp.dot(a, b, precision=precision, preferred_element_type=F32)


def mm_t(a, b, precision=None):
    return lax.dot_general(
        a, b, (((1,), (1,)), ((), ())), precision=precision, preferred_element_type=F32
    )


def split(x):
    high = x.astype(BF16)
    return high, (x - high.astype(F32)).astype(BF16)


def mm_split(a, b, product=mm):
    (ah, al), (bh, bl) = a, b
    return product(ah, bh) + (product(ah, bl) + product(al, bh))


def mm_low(a, b):
    return mm(a.astype(BF16), b.astype(BF16))


PIECES = 3


def heads_kernel(
    own, t_own, out, px_out, sx_out, t_out, mz_out, t_all, p_own, p_all,
    l_sem, p_s, p_r, a_s, a_r, f_s, f_r, ts, tr, zs, zr,
):
    ctx, head, z, place, y_hi, x, y_lo, core = coords()
    partner = (ctx, y_lo * 2 + 1 - core)
    across = (ctx, (1 - y_lo) * 2 + core)
    plane = [(z * 8 + lax.rem(place + d, 8), head) for d in range(1, 8)]
    column = [(lax.rem(z + d, 8) * 8 + place, head) for d in range(1, 8)]
    greet([partner, across] + plane + column)
    size = ROWS // PIECES

    def part(i, h):
        return out.at[pl.ds(i * size, size), pl.ds(pl.multiple_of(h * 1024, 1024), 1024)]

    def piece(i):
        return own.at[pl.ds(i * size, size)]

    far, farther = (1 - y_lo) * 2 + core, (1 - y_lo) * 2 + 1 - core
    sends = []
    for d in range(1, 8):
        owner = lax.rem(place + d, 8)
        copy = push(t_own.at[owner], t_all.at[8 - d], ts.at[d - 1], tr.at[7 - d], plane[d - 1])
        copy.start()
        sends.append(copy)
    keep = [pltpu.make_async_copy(piece(i), part(i, head), l_sem.at[i]) for i in range(PIECES)]
    for i in range(PIECES):
        push(piece(i), part(i, head), a_s.at[i], a_r.at[i], across).start()
        push(piece(i), part(i, head), p_s.at[i], p_r.at[i], partner).start()
        keep[i].start()

    def pass_on(i):
        push(piece(i), part(i, far), a_s.at[i], a_r.at[i], across).wait_recv()
        push(part(i, far), part(i, far), f_s.at[i], f_r.at[i], partner).start()

    unit_k = jnp.where(
        lax.broadcasted_iota(jnp.int32, (128, 128), 0)
        == lax.broadcasted_iota(jnp.int32, (128, 128), 1),
        1.0,
        0.0,
    )
    t_all[0] = t_own[place]
    for d in range(1, 8):
        push(t_own.at[0], t_all.at[8 - d], ts.at[d - 1], tr.at[7 - d], plane[d - 1]).wait_recv()
    pass_on(0)
    for i in range(8):
        t_out[i] = t_all[lax.rem(i - place + 8, 8)]
    before, after = unit_k, unit_k
    for i in range(8):
        px_out[i] = before.astype(BF16)
        high, low = split(before)
        before = mm(t_out[i], high) + mm(t_out[i], low)
        j = 7 - i
        sx_out[:, j * 128 : (j + 1) * 128] = after.astype(BF16)
        if j > 0:
            high, low = split(after)
            after = mm(high, t_out[j]) + mm(low, t_out[j])
        if i == 4:
            pass_on(1)
    p_own[...] = before.astype(BF16)
    for d in range(1, 8):
        copy = push(p_own, p_all.at[d - 1], zs.at[d - 1], zr.at[d - 1], column[d - 1])
        copy.start()
        sends.append(copy)
    pass_on(2)
    for d in range(1, 8):
        push(p_own, p_all.at[d - 1], zs.at[d - 1], zr.at[d - 1], column[d - 1]).wait_recv()
    running = unit_k
    for r in range(1, 8):
        valid = z >= r
        mz_out[:, (r - 1) * 128 : r * 128] = jnp.where(valid, running, 0.0).astype(BF16)
        if r < 7:
            high, low = split(running)
            running = mm(high, p_all[r - 1]) + mm(low, p_all[r - 1])
    for i in range(PIECES):
        near = y_lo * 2 + 1 - core
        push(piece(i), part(i, near), p_s.at[i], p_r.at[i], partner).wait()
        push(part(i, far), part(i, farther), f_s.at[i], f_r.at[i], partner).wait()
        push(piece(i), part(i, far), a_s.at[i], a_r.at[i], across).wait_send()
        keep[i].wait()
    for copy in sends:
        copy.wait_send()


def all_heads(own, transitions):
    dma = pltpu.SemaphoreType.DMA
    vmem = pl.BlockSpec(memory_space=pltpu.VMEM)
    return pl.pallas_call(
        heads_kernel,
        out_shape=(
            jax.ShapeDtypeStruct((ROWS, 4096), BF16),
            jax.ShapeDtypeStruct((8, 128, 128), BF16),
            jax.ShapeDtypeStruct((128, 1024), BF16),
            jax.ShapeDtypeStruct((8, 128, 128), BF16),
            jax.ShapeDtypeStruct((128, 896), BF16),
        ),
        in_specs=[vmem] * 2,
        out_specs=[pl.BlockSpec(memory_space=pl.ANY)] + [vmem] * 4,
        scratch_shapes=[
            pltpu.VMEM((8, 128, 128), BF16),
            pltpu.VMEM((128, 128), BF16),
            pltpu.VMEM((7, 128, 128), BF16),
        ]
        + [dma((PIECES,))] * 7
        + [dma((7,))] * 4,
        compiler_params=pltpu.CompilerParams(collective_id=1, has_side_effects=True),
        name="all_heads",
    )(own, transitions)


def causal(ext, taps, width):
    total = jnp.zeros((ROWS, width), F32)
    taps = taps[...].astype(F32)
    for m in range(4):
        total = total + taps[m : m + 1, :] * ext[13 + m : 13 + m + ROWS, 0:width]
    return total / (1.0 + jnp.exp(-total))


def triangle(size, strict):
    row = lax.broadcasted_iota(jnp.int32, (size, size), 0)
    col = lax.broadcasted_iota(jnp.int32, (size, size), 1)
    return (col < row) if strict else (col <= row)


def inverse_lower(systems):
    row = lax.broadcasted_iota(jnp.int32, (ROWS, ROWS), 0)
    col = lax.broadcasted_iota(jnp.int32, (ROWS, ROWS), 1)
    unit = jnp.where(row == col, 1.0, 0.0)
    block = lax.div(row, 8) == lax.div(col, 8)
    powers = [jnp.where(block, -m, 0.0) for m in systems]
    inverses = [unit + p for p in powers]
    for _ in range(2):
        powers = [mm_low(p, p) for p in powers]
        inverses = [x + mm_low(x, p) for x, p in zip(inverses, powers)]
    size = 8
    while size < ROWS:
        pair = 2 * size
        below = (lax.div(row, pair) == lax.div(col, pair)) & (lax.div(row, size) != lax.div(col, size))
        if pair >= ROWS:
            below = lax.div(row, size) != lax.div(col, size)
        lows = [x.astype(BF16) for x in inverses]
        inner = [
            mm(jnp.where(below, m, 0.0).astype(BF16), x) for m, x in zip(systems, lows)
        ]
        inverses = [
            x - mm(low, i.astype(BF16)) for x, low, i in zip(inverses, lows, inner)
        ]
        size = pair
        yield None
    splits = [split(x) for x in inverses]
    rests = [
        (unit - x) - mm_split(split(m), xs) for m, x, xs in zip(systems, inverses, splits)
    ]
    yield [x + mm(xs[0], r.astype(BF16)) for x, xs, r in zip(inverses, splits, rests)]


def linear_kernel(
    lq, lk, cq, ck, decay_logits, beta_logits, decay_base, decay_bias, keys, values, seg,
    h_out, eff_out, g_out, t_own, kv, segs,
    own, own_seg, w_load, wy_s, wy_r, wz_s, wz_r, wx_s, wx_r, wf_s, wf_r,
    halo, ext, q_sc, k_sc, row_sc, hs, hr,
):
    ctx, head, z, place, y_hi, x, y_lo, core = coords()
    following = (lax.rem(ctx + 1, 64), head)
    previous = (lax.rem(ctx + 63, 64), head)
    transfers = window_steps(
        keys, values, seg, kv, segs, own, own_seg, w_load,
        wy_s, wy_r, wz_s, wz_r, wx_s, wx_r, wf_s, wf_r,
    )
    next(transfers)
    greet([previous] + window_sources())
    tail = pl.ds(ROWS - 16, 16)
    edge = [
        push(lq.at[tail], halo.at[0], hs.at[0], hr.at[0], following),
        push(lk.at[tail], halo.at[1], hs.at[1], hr.at[1], following),
    ]
    for copy in edge:
        copy.start()
    next(transfers)
    for copy in edge:
        copy.wait()
    begins = ctx == 0
    for source, taps, index, target in ((lq, cq, 0, q_sc), (lk, ck, 1, k_sc)):
        ext[0:16, :] = jnp.where(begins, 0.0, halo[index].astype(F32))
        ext[16 : 16 + ROWS, :] = source[...].astype(F32)
        conv = causal(ext, taps, 512)
        for n in range(4):
            part = conv[:, n * 128 : (n + 1) * 128]
            part = part / jnp.sqrt(jnp.sum(part * part, axis=1, keepdims=True) + EPSILON)
            if index == 0:
                part = part * (1.0 / 128.0**0.5)
            target[n] = part
        next(transfers)
    lower = triangle(ROWS, False)
    strict = triangle(ROWS, True)
    ones = jnp.where(lower, 1.0, 0.0)
    row = lax.broadcasted_iota(jnp.int32, (ROWS, ROWS), 0)
    col = lax.broadcasted_iota(jnp.int32, (ROWS, ROWS), 1)
    unit = jnp.where(row == col, 1.0, 0.0)
    unit_k = jnp.where(
        lax.broadcasted_iota(jnp.int32, (128, 128), 0)
        == lax.broadcasted_iota(jnp.int32, (128, 128), 1),
        1.0,
        0.0,
    )
    same = lax.broadcasted_iota(jnp.int32, (HEADS, HEADS), 0) == lax.broadcasted_iota(
        jnp.int32, (HEADS, HEADS), 1
    )
    base = jnp.sum(jnp.where(same, decay_base[...], 0.0), axis=1, keepdims=True)
    bias = jnp.sum(jnp.where(same, decay_bias[...], 0.0), axis=1, keepdims=True)
    shifted = decay_logits[...] + bias
    softplus = jnp.maximum(shifted, 0.0) + jnp.log1p(jnp.exp(-jnp.abs(shifted)))
    decay = -jnp.exp(base) * softplus
    beta = jax.nn.sigmoid(beta_logits[...])
    row_sc[0] = mm_t(decay, ones, HIGH)
    row_sc[1] = beta
    sum_col = mm_t(ones, decay, HIGH)
    beta_col = mm_t(unit, beta, HIGH)
    group = 2
    for base in range(0, HEADS, group):
        parts, systems = [], []
        for e in range(base, base + group):
            q, k = q_sc[e // 2], k_sc[e // 2]
            if e % 2 == 0:
                k_split = split(k)
                key_key = mm_split(k_split, k_split, mm_t)
                query_key = mm_split(split(q), k_split, mm_t)
            c_col, c_row = sum_col[:, e : e + 1], row_sc[0, e : e + 1, :]
            b_col, b_row = beta_col[:, e : e + 1], row_sc[1, e : e + 1, :]
            fade = jnp.exp(jnp.where(lower, c_col - c_row, NEGATIVE))
            systems.append(jnp.where(strict, b_col * key_key * fade, 0.0))
            parts.append((q, k, c_col, b_col, b_row, query_key * fade))
        for inverses in inverse_lower(systems):
            pass
        for e, inverse, (q, k, c_col, b_col, b_row, scores) in zip(
            range(base, base + group), inverses, parts
        ):
            grown = jnp.exp(c_col)
            inverse = split(inverse)
            scores = split(scores)
            weight_keys = split(mm_split(inverse, split((b_col * grown) * k)))
            eff_out[e] = (grown * q - mm_split(scores, weight_keys)).astype(BF16)
            h_out[e] = (mm_split(scores, inverse) * b_row).astype(BF16)
            final = c_col[ROWS - 1 : ROWS, :]
            decayed = split(jnp.transpose(jnp.exp(final - c_col) * k))
            t_own[e] = (jnp.exp(final) * unit_k - mm_split(decayed, weight_keys)).astype(BF16)
            g_out[e] = (mm_split(decayed, inverse) * b_row).astype(BF16)
        next(transfers, None)
    for _ in transfers:
        pass


def linear(*operands):
    dma = pltpu.SemaphoreType.DMA
    vmem = pl.BlockSpec(memory_space=pltpu.VMEM)
    anywhere = pl.BlockSpec(memory_space=pl.ANY)
    return pl.pallas_call(
        linear_kernel,
        out_shape=(
            jax.ShapeDtypeStruct((HEADS, ROWS, ROWS), BF16),
            jax.ShapeDtypeStruct((HEADS, ROWS, 128), BF16),
            jax.ShapeDtypeStruct((HEADS, 128, ROWS), BF16),
            jax.ShapeDtypeStruct((HEADS, 128, 128), BF16),
            jax.ShapeDtypeStruct((3, 2, 4, ROWS, 512), BF16),
            jax.ShapeDtypeStruct((4, 3, 2, 8, 128), jnp.int32),
        ),
        in_specs=[vmem] * 8 + [anywhere] * 3,
        out_specs=[vmem] * 4 + [anywhere] * 2,
        scratch_shapes=[
            pltpu.VMEM((2, ROWS, 512), BF16),
            pltpu.VMEM((8, 128), jnp.int32),
            dma((7,)),
            dma((2,)),
            dma((2,)),
            dma((6,)),
            dma((6,)),
            dma((3, 5)),
            dma((3, 5)),
            dma((17,)),
            dma((17,)),
            pltpu.VMEM((2, 16, 512), BF16),
            pltpu.VMEM((16 + ROWS, 512), F32),
            pltpu.VMEM((4, ROWS, 128), F32),
            pltpu.VMEM((4, ROWS, 128), F32),
            pltpu.VMEM((2, HEADS, ROWS), F32),
            dma((2,)),
            dma((2,)),
        ],
        compiler_params=pltpu.CompilerParams(collective_id=2, has_side_effects=True),
        name="linear_operators",
    )(*operands)


def delta_kernel(
    value_in, cv, h_in, eff_in, g_in, px_in, sx_in, t_in, mz_in, attn, gate, gain, rezero, out,
    halo, ext, v_sc, b_own, b_all, local, gated_sc, l_own, l_all, within, s_own, s_all,
    hs, hr, bs, br, zs, zr, ss, sr,
):
    ctx, head, z, place, y_hi, x, y_lo, core = coords()
    following = (lax.rem(ctx + 1, 64), head)
    previous = (lax.rem(ctx + 63, 64), head)
    plane = [(z * 8 + lax.rem(place + d, 8), head) for d in range(1, 8)]
    column = [(lax.rem(z + d, 8) * 8 + place, head) for d in range(1, 8)]
    greet([previous] + plane + column)
    edge = push(value_in.at[pl.ds(ROWS - 16, 16)], halo, hs.at[0], hr.at[0], following)
    edge.start()
    ext[16 : 16 + ROWS, :] = value_in[...].astype(F32)
    edge.wait()
    ext[0:16, :] = jnp.where(ctx == 0, 0.0, halo[...].astype(F32))
    v_sc[...] = causal(ext, cv, 1024).astype(BF16)
    for e in range(HEADS):
        b_own[e] = mm(g_in[e], v_sc[:, e * 128 : (e + 1) * 128]).astype(BF16)
    sends = []
    for d in range(1, 8):
        owner = lax.rem(place + d, 8)
        copy = push(b_own.at[owner], b_all.at[place], bs.at[d - 1], br.at[d - 1], plane[d - 1])
        copy.start()
        sends.append(copy)
    b_all[place] = b_own[place]
    for e in range(HEADS):
        local[e] = mm(h_in[e], v_sc[:, e * 128 : (e + 1) * 128])
    for d in range(1, 8):
        source = lax.rem(place + 8 - d, 8)
        push(b_own.at[0], b_all.at[source], bs.at[d - 1], br.at[d - 1], plane[d - 1]).wait_recv()
    blocks = b_all[...].reshape(8 * 128, 128)
    l_own[...] = mm(sx_in[...], blocks).astype(BF16)
    for d in range(1, 8):
        copy = push(l_own, l_all.at[d - 1], zs.at[d - 1], zr.at[d - 1], column[d - 1])
        copy.start()
        sends.append(copy)
    within[0] = jnp.zeros((128, 128), F32)
    running = b_all[0].astype(F32)
    within[1] = running
    for i in range(1, 7):
        high, low = split(running)
        running = mm(t_in[i], high) + mm(t_in[i], low) + b_all[i].astype(F32)
        within[i + 1] = running
    for e in range(HEADS):
        cols = slice(e * 128, (e + 1) * 128)
        g = gate[:, cols].astype(F32)
        gated_sc[e] = rezero[:, cols] * gain[...] * (g * jax.nn.sigmoid(g))
    for d in range(1, 8):
        push(l_own, l_all.at[d - 1], zs.at[d - 1], zr.at[d - 1], column[d - 1]).wait_recv()
    entry = mm(mz_in[...], l_all[...].reshape(7 * 128, 128)).astype(BF16)
    for i in range(8):
        s_own[i] = (mm(px_in[i], entry) + within[i]).astype(BF16)
    for d in range(1, 8):
        target = lax.rem(place + d, 8)
        copy = push(s_own.at[target], s_all.at[place], ss.at[d - 1], sr.at[d - 1], plane[d - 1])
        copy.start()
        sends.append(copy)
    s_all[place] = s_own[place]
    for d in range(1, 8):
        source = lax.rem(place + 8 - d, 8)
        push(s_own.at[0], s_all.at[source], ss.at[d - 1], sr.at[d - 1], plane[d - 1]).wait_recv()
    for e in range(HEADS):
        cols = slice(e * 128, (e + 1) * 128)
        delta = local[e] + mm(eff_in[e], s_all[e])
        norm = delta / jnp.sqrt(jnp.mean(delta * delta, axis=1, keepdims=True) + EPSILON)
        out[:, cols] = (attn[:, cols].astype(F32) + norm * gated_sc[e]).astype(BF16)
    for copy in sends:
        copy.wait_send()


def delta(value_in, cv, ops, attn, gate, gain, rezero):
    dma = pltpu.SemaphoreType.DMA
    vmem = pl.BlockSpec(memory_space=pltpu.VMEM)
    return pl.pallas_call(
        delta_kernel,
        out_shape=jax.ShapeDtypeStruct((ROWS, 1024), BF16),
        in_specs=[vmem] * 13,
        out_specs=vmem,
        scratch_shapes=[
            pltpu.VMEM((16, 1024), BF16),
            pltpu.VMEM((16 + ROWS, 1024), F32),
            pltpu.VMEM((ROWS, 1024), BF16),
            pltpu.VMEM((8, 128, 128), BF16),
            pltpu.VMEM((8, 128, 128), BF16),
            pltpu.VMEM((8, ROWS, 128), F32),
            pltpu.VMEM((8, ROWS, 128), F32),
            pltpu.VMEM((128, 128), BF16),
            pltpu.VMEM((7, 128, 128), BF16),
            pltpu.VMEM((8, 128, 128), F32),
            pltpu.VMEM((8, 128, 128), BF16),
            pltpu.VMEM((8, 128, 128), BF16),
            dma((1,)),
            dma((1,)),
            dma((7,)),
            dma((7,)),
            dma((7,)),
            dma((7,)),
            dma((7,)),
            dma((7,)),
        ],
        compiler_params=pltpu.CompilerParams(collective_id=3, has_side_effects=True),
        name="delta_rule",
    )(value_in, cv, *ops, attn, gate, gain, rezero)


def body(
    queries,
    attention_keys,
    attention_values,
    attn_gate,
    segment_ids,
    value_proj,
    linear_queries,
    linear_keys,
    conv_queries,
    conv_keys,
    conv_values,
    decay_logits,
    beta_logits,
    decay_base,
    decay_bias,
    output_gate,
    output_gain,
    rezero_gate,
):
    ctx = lax.axis_index("ctx")
    seg_tile = jnp.pad(segment_ids, (0, 1024 - ROWS), constant_values=127).reshape(8, 128)
    *ops, transitions, kv, segs = linear(
        linear_queries,
        linear_keys,
        conv_queries,
        conv_keys,
        decay_logits.T,
        beta_logits.T,
        decay_base.reshape(1, HEADS),
        decay_bias.reshape(1, HEADS),
        attention_keys,
        attention_values,
        seg_tile,
    )
    back = 16 - jnp.arange(WINDOW, dtype=jnp.int32)
    source = ctx - back + 64
    step = source // 8
    step = (ctx + 64) // 8 - step
    y_hi, x = (source // 4) % 2, source % 4
    missing = jnp.maximum(16 - ctx, 0).astype(jnp.int32).reshape(1)
    slots = jnp.concatenate(
        [step * 8 + y_hi * 4 + x, x * 6 + step * 2 + y_hi, missing]
    ).astype(jnp.int32)
    seg_query = jnp.concatenate([segment_ids.reshape(1, ROWS)] * 4, axis=1)
    attn_out = attention(
        slots, kv.reshape(24, ROWS, 512), segs.reshape(24, 8, 128), seg_query, queries, attn_gate
    )
    everything, *scan = all_heads(attn_out, transitions)
    squares = jnp.mean(jnp.square(everything.astype(F32)), axis=1, keepdims=True)
    summed = jnp.dot(everything, value_proj, preferred_element_type=F32)
    value_in = (summed / jnp.sqrt(squares + EPSILON)).astype(BF16)
    return delta(
        value_in,
        conv_values,
        (*ops, *scan),
        attn_out,
        output_gate,
        output_gain.reshape(1, 128),
        rezero_gate.reshape(1, 1024),
    )


def solution(mesh):
    placed = (
        P("ctx", "head"),
        P("ctx", None),
        P("ctx", None),
        P("ctx", "head"),
        P("ctx"),
        P(None, "head"),
        P("ctx", "head"),
        P("ctx", "head"),
        P(None, "head"),
        P(None, "head"),
        P(None, "head"),
        P("ctx", "head"),
        P("ctx", "head"),
        P("head"),
        P("head"),
        P("ctx", "head"),
        P(),
        P("head"),
    )
    return jax.shard_map(
        body, mesh=mesh, in_specs=placed, out_specs=P("ctx", "head"), check_vma=False
    )
```
